1024 devices in a mesh: ia: 64 (over x, z_hi, y), ja: 16 (over z_lo, core).
Axes of the slice: x: 4, y: 8, z: 16 (z_hi: 2, z_lo: 8; z = z_hi * 8 + z_lo), core: 2. Of those that a mesh axis runs over, the one named last changes fastest.
Arguments:
- b_first: bfloat16 [64, 512, 1024], P('ia', None, 'ja'), may hold values from -0.63671875 to 0.63671875
- b_second: bfloat16 [32, 512, 1024], P('ja', None, 'ia'), may hold values from -0.63671875 to 0.63671875
- eps_first: float32 [64], P('ia'), may hold values from -2 to -0.3
- eps_second: float32 [32], P('ja'), may hold values from -2 to -0.3
- eps_virtual: float32 [512], replicated, may hold values from 0.1 to 3
- c_virtual: float32 [576, 512], replicated, may hold values from -0.25 to 0.25
- c_occupied: float32 [64, 576], replicated, may hold values from -0.75 to 0.75
Outputs:
- gamma_ao: float32 [576, 589824], P('ia', 'ja')
- density: float32 [512, 512], P('ia', 'ja')
The draws below stay inside these ranges and needn't reach their ends.
All inputs are finite; a program needn't handle non-finite values.
Results may differ from the reference program's by a relative error of at most 0.0008.
Values may be sent and summed in bfloat16 or wider, within the bound.
A program may use at most 32 MiB of HBM per device.

```python
import math
import jax
import jax.numpy as jnp
from jax import lax

NV = 512
NAUX = 1024
NBF = 576
NI = 64
NJ = 32


def levels(stream_key, extent, pieces, least, top_value):
    gain, own = 1.0, jax.random.fold_in(stream_key, 6)
    for position, blocks in pieces:
        draws = jnp.exp(jax.random.uniform(jax.random.fold_in(own, position), (blocks,), jnp.float32, least / len(pieces), top_value / len(pieces)))
        gain = gain * jnp.repeat(draws, extent[position] // blocks).reshape([-1 if axis == position else 1 for axis in range(len(extent))])
    return gain


def gaussian(rng, dims, deviation, most, pieces=(), kind=jnp.bfloat16):
    array = deviation * jax.random.normal(rng, dims, jnp.float32)
    if pieces:
        array = array * levels(rng, dims, pieces, -0.22, 0.18)
    return jnp.clip(array, -most, most).astype(kind)


def setup_inputs(seed: int = 0) -> dict:
    streams_of = jax.random.split(jax.random.key(seed), 8)
    return {
        "b_first": gaussian(streams_of[0], (NI, NV, NAUX), 0.08, 0.63671875, ((0, 64), (2, 16))),
        "b_second": gaussian(streams_of[1], (NJ, NV, NAUX), 0.08, 0.63671875, ((0, 16), (2, 64))),
        "eps_first": jnp.clip(-2.0 + 1.7 * jax.random.uniform(streams_of[2], (NI,), jnp.float32) ** levels(streams_of[2], (NI,), ((0, 64),), -0.2, 0.2), -2.0, -0.3),
        "eps_second": jnp.clip(-2.0 + 1.7 * jax.random.uniform(streams_of[3], (NJ,), jnp.float32) ** levels(streams_of[3], (NJ,), ((0, 16),), -0.2, 0.2), -2.0, -0.3),
        "eps_virtual": jnp.clip(jnp.exp(jax.random.uniform(streams_of[4], (NV,), jnp.float32, math.log(0.1), math.log(3.0))), 0.1, 3.0),
        "c_virtual": gaussian(streams_of[5], (NBF, NV), NV ** -0.5, 0.25, (), jnp.float32),
        "c_occupied": gaussian(streams_of[6], (NI, NBF), NI ** -0.5, 0.75, (), jnp.float32),
    }


def round_keep(values):
    return lax.optimization_barrier(values.astype(jnp.bfloat16)).astype(jnp.float32)


def reference(b_first, b_second, eps_first, eps_second, eps_virtual, c_virtual, c_occupied):
    second = b_second.astype(jnp.float32)

    def per_first(inputs):
        block, energy = inputs
        integrals = jnp.einsum('ap,jbp->jab', block.astype(jnp.float32), second)
        denominator = (eps_virtual[None, :, None] + eps_virtual[None, None, :]
                       - energy - eps_second[:, None, None])
        amplitude = integrals / (-denominator)
        tilde = round_keep(2.0 * amplitude - jnp.swapaxes(amplitude, 1, 2))
        amp_round = round_keep(amplitude)
        gamma_row = jnp.einsum('jab,jbp->ap', tilde, second)
        density_row = jnp.einsum('jac,jbc->ab', tilde, amp_round)
        return gamma_row, density_row

    gamma_mo, density_rows = lax.map(per_first, (b_first, eps_first))
    density = jnp.sum(density_rows, axis=0) / (NI * NJ)
    virtual_back = jnp.einsum('na,iap->inp', c_virtual, gamma_mo, precision=lax.Precision.HIGHEST)
    gamma_ao = jnp.einsum('im,inp->npm', c_occupied, virtual_back, precision=lax.Precision.HIGHEST)
    gamma_ao = gamma_ao.reshape(NBF, NAUX * NBF)
    return gamma_ao, density
```

```python
import jax
import jax.numpy as jnp
from jax import lax
from jax.experimental import pallas as pl
from jax.experimental.pallas import tpu as pltpu
from jax.sharding import PartitionSpec as P

F32, BF16 = jnp.float32, jnp.bfloat16
MESH = pl.DeviceIdType.MESH
NX, NY, NH, NL, NZ = 4, 8, 2, 8, 16
PLANE = NX * NY
CR = 72
BR = 9


def dot(a, b, ca, cb):
    return lax.dot_general(a, b, (((ca,), (cb,)), ((), ())), preferred_element_type=F32)


def split(v):
    hi = v.astype(BF16)
    return hi, (v - hi.astype(F32)).astype(BF16)


def place():
    ia, ja = lax.axis_index("ia"), lax.axis_index("ja")
    return ia // 16, (ia // 8) % 2, ia % 8, ja // 2, ja % 2


def dev(x, y, z, c):
    return ((x * 2 + z // 8) * 8 + y, (z % 8) * 2 + c)


def remote(src, dst, ss, rs, to):
    return pltpu.make_async_remote_copy(
        src_ref=src, dst_ref=dst, send_sem=ss, recv_sem=rs, device_id=to, device_id_type=MESH
    )


def main_kernel(
    bf, bs, e1, e2, ev, cv,
    R, dens_out,
    F, S, E, Chi, Clo, T, AR, Ghi, Glo, D, DP, DY, DX, DZ, DR, DO, QR, QL, SB,
    f0_s, f0_r, fr_s, fr_r, fl_s, fl_r,
    w_s, w_r, sx_s, sx_r, yr_s, yr_r, yl_s, yl_r, pc_s, pc_r, e_s, e_r,
    qr_s, qr_r, ql_s, ql_r, dp_s, dp_r, dy_s, dy_r, dx_s, dx_r, dz_s, dz_r, do_s, do_r,
    a_s, a_r, r_s, r_r, loc,
):
    x, h, y, l, c = place()
    z = h * 8 + l
    k = 1 - c
    ip = x * 8 + y
    ja = l * 2 + c
    home = c == h
    mate = dev(x, y, z, k)
    far = lax.rem(z + 8, NZ)

    E[0, 0] = jnp.full((8, 128), e1[0], F32)
    E[0, 1] = jnp.full((8, 128), e2[0], F32)
    E[0, 2] = jnp.full((8, 128), e2[1], F32)
    barrier = pltpu.get_barrier_semaphore()

    def hail(to):
        pl.semaphore_signal(barrier, inc=1, device_id=to, device_id_type=MESH)

    hail(mate)
    hail(dev(x, y, far, k))

    @pl.loop(1, NZ)
    def _(d):
        hail(dev(x, y, lax.rem(z + d, NZ), c))

    @pl.loop(1, PLANE)
    def _(d):
        q = lax.rem(ip + d, PLANE)
        hail(dev(q // 8, q % 8, z, c))

    pl.semaphore_wait(barrier, 2 + NZ - 1 + PLANE - 1)

    e_far = remote(E.at[0], E.at[1], e_s.at[0], e_r.at[0], dev(x, y, far, c))
    e_mate = remote(E.at[0], E.at[2], e_s.at[1], e_r.at[1], mate)
    s_own = [S.at[j, x, h, y] for j in range(2)]

    @pl.when(home)
    def _():
        remote(bs.at[k], S.at[k, x, h, y], w_s.at[0], w_r.at[0], mate).start()
        pltpu.make_async_copy(bs.at[c], S.at[c, x, h, y], loc.at[0]).start()
        pltpu.make_async_copy(bf, F.at[ja], loc.at[1]).start()

    @pl.when(jnp.logical_not(home))
    def _():
        remote(bf, F.at[ja], f0_s, f0_r, mate).start()
        remote(bs.at[c], S.at[c, x, h, y], w_s.at[0], w_r.at[1], dev(x, y, far, c)).start()
        remote(bs.at[k], S.at[k, x, h, y], w_s.at[1], w_r.at[1], dev(x, y, far, k)).start()

    e_far.start()
    e_mate.start()

    def split_c(g):
        hi, lo = split(cv[g])
        Chi[g] = hi
        Clo[g] = lo

    pl.loop(0, 8)(split_c)

    def x_sends(hp, slot):
        for d in range(1, NX):
            to = lax.rem(x + d, NX)
            piece = S.at[c, x, hp, y]
            remote(piece, piece, sx_s.at[slot, d - 1], sx_r.at[slot, d - 1], dev(to, y, z, c)).start()

    def x_waits(hp, slot):
        for d in range(1, NX):
            frm = lax.rem(x + NX - d, NX)
            piece = S.at[c, frm, hp, y]
            remote(piece, piece, sx_s.at[slot, d - 1], sx_r.at[slot, d - 1], mate).wait_recv()
        for d in range(1, NX):
            piece = S.at[c, x, hp, y]
            remote(piece, piece, sx_s.at[slot, d - 1], sx_r.at[slot, d - 1], mate).wait_send()

    yr, yl = lax.rem(y + 1, NY), lax.rem(y + NY - 1, NY)

    def y_block(hp, yo):
        return S.at[c, :, hp, yo]

    def y_copy(hp, slot, s, right):
        yo = lax.rem(y + NY - s, NY) if right else lax.rem(y + s, NY)
        b = y_block(hp, yo)
        ss, rs = (yr_s, yr_r) if right else (yl_s, yl_r)
        return remote(b, b, ss.at[slot, s], rs.at[slot, s], dev(x, yr if right else yl, z, c))

    def y_got(hp, slot, s, right):
        yo = lax.rem(y + NY - s, NY) if right else lax.rem(y + s, NY)
        b = y_block(hp, yo)
        ss, rs = (yr_s, yr_r) if right else (yl_s, yl_r)
        remote(b, b, ss.at[slot, s - 1], rs.at[slot, s - 1], mate).wait_recv()

    def share(hp, slot, n, yo):
        b = y_block(hp, yo)
        remote(b, b, pc_s.at[slot, n], pc_r.at[slot, n], mate).start()

    def y_step(hp, slot, s):
        if s == 0:
            y_copy(hp, slot, 0, True).start()
            y_copy(hp, slot, 0, False).start()
            share(hp, slot, 0, y)
            return
        y_got(hp, slot, s, True)
        if s < 4:
            y_copy(hp, slot, s, True).start()
        share(hp, slot, s, lax.rem(y + NY - s, NY))
        if s < 4:
            y_got(hp, slot, s, False)
            if s < 3:
                y_copy(hp, slot, s, False).start()
            share(hp, slot, 4 + s, lax.rem(y + s, NY))

    zr, zl = lax.rem(z + 1, NZ), lax.rem(z + NZ - 1, NZ)

    def f_step(s):
        for right in (True, False):
            last = 8 if right else 7
            if s > last:
                continue
            o = lax.rem(z + NZ - s, NZ) if right else lax.rem(z + s, NZ)
            ss, rs = (fr_s, fr_r) if right else (fl_s, fl_r)
            to = dev(x, y, zr if right else zl, c)

            @pl.when(o // 8 == c)
            def _():
                for q in range(2):
                    b = F.at[lax.rem(o, NL) * 2 + q]
                    if s > 0:
                        remote(b, b, ss.at[s - 1, q], rs.at[s - 1, q], to).wait_recv()
                    if s < last:
                        remote(b, b, ss.at[s, q], rs.at[s, q], to).start()

    @pl.when(home)
    def _():
        pltpu.make_async_copy(bs.at[c], S.at[c, x, h, y], loc.at[0]).wait()
        pltpu.make_async_copy(bf, F.at[ja], loc.at[1]).wait()
        remote(bf, F.at[l * 2 + k], f0_s, f0_r, mate).wait_recv()

    @pl.when(jnp.logical_not(home))
    def _():
        remote(bs.at[c], S.at[c, x, h, y], w_s.at[0], w_r.at[0], mate).wait_recv()

    other = 1 - h
    x_sends(h, 0)
    f_step(0)
    x_waits(h, 0)
    y_step(h, 0, 0)
    f_step(1)
    y_step(h, 0, 1)
    f_step(2)
    y_step(h, 0, 2)
    remote(bs.at[c], S.at[c, x, other, y], w_s.at[0], w_r.at[1], mate).wait_recv()
    x_sends(other, 1)
    f_step(3)
    y_step(h, 0, 3)
    x_waits(other, 1)
    y_step(other, 1, 0)
    f_step(4)
    y_step(h, 0, 4)
    y_step(other, 1, 1)
    f_step(5)
    y_step(other, 1, 2)
    f_step(6)
    y_step(other, 1, 3)
    f_step(7)
    y_step(other, 1, 4)
    f_step(8)

    e_far.wait()
    e_mate.wait()
    for slot, hp in ((0, h), (1, other)):
        for n in range(NY):
            b = S.at[k, :, hp, n]
            remote(b, b, pc_s.at[slot, n], pc_r.at[slot, n], mate).wait_recv()

    ei = jnp.where(home, E[0, 0, 0:1, 0:1], E[1, 0, 0:1, 0:1])
    row = ev[...]
    for j in range(2):
        ej = jnp.where(home, E[0, 1 + j, 0:1, 0:1], E[2, 1 + j, 0:1, 0:1])

        @pl.loop(0, 4)
        def _(t):
            cols = pl.ds(pl.multiple_of(t * 128, 128), 128)
            full_s = S[j].reshape(1024, 512)
            full_f = F[...].reshape(1024, 512)
            tile_f = F[:, :, cols].reshape(1024, 128)
            tile_s = S[j, :, :, :, :, cols].reshape(1024, 128)
            i_ab = dot(tile_f, full_s, 0, 0)
            i_ba = dot(tile_s, full_f, 0, 0)
            col = jnp.transpose(jnp.broadcast_to(ev[:, cols], (128, 128)))[:, 0:1]
            r = 1.0 / (ei + ej - (col + row))
            a = i_ab * r
            at = i_ba * r
            rows = pl.ds(pl.multiple_of(t * 128, 128), 128)
            T[j, rows, :] = (2.0 * a - at).astype(BF16)
            AR[j, rows, :] = at.astype(BF16)

    @pl.loop(0, 8)
    def _(g):
        gx, gh = g // 2, g % 2
        acc = dot(T[0], S[0, gx, gh].reshape(128, 512), 1, 1)
        acc += dot(T[1], S[1, gx, gh].reshape(128, 512), 1, 1)
        hi, lo = split(acc)
        Ghi[g] = hi
        Glo[g] = lo

    def own(d, q):
        hd, ld = d // 8, d % 8
        ghi, glo = Ghi[ld], Glo[ld]
        out = []
        for xi in (2 * q, 2 * q + 1):
            chi, clo = Chi[xi * 2 + hd], Clo[xi * 2 + hd]
            out.append(dot(chi, ghi, 1, 0) + dot(clo, ghi, 1, 0) + dot(chi, glo, 1, 0))
        return jnp.concatenate(out, axis=0)

    def q_copy(buf, s, q, right):
        ss, rs = (qr_s, qr_r) if right else (ql_s, ql_r)
        return remote(
            buf.at[s, q], buf.at[s + 1, q], ss.at[s, q], rs.at[s, q], dev(x, y, zr if right else zl, c)
        )

    for right, buf in ((True, QR), (False, QL)):
        d0 = lax.rem(z + (8 if right else 9), NZ)
        for q in range(2):
            buf[0, q] = own(d0, q)
            q_copy(buf, 0, q, right).start()

    def q_steps(lo, hi):
        @pl.loop(lo, hi)
        def _(s):
            dr = lax.rem(z + 8 + NZ - s, NZ)
            dl = lax.rem(z + 9 + s, NZ)
            for right, buf, d in ((True, QR, dr), (False, QL, dl)):
                for q in range(2):
                    mine = own(d, q)
                    q_copy(buf, s - 1, q, right).wait_recv()
                    buf[s, q] += mine
                    q_copy(buf, s, q, right).start()

    for t in range(4):
        acc = dot(T[0, t * 128 : t * 128 + 128, :], AR[0], 1, 0)
        acc += dot(T[1, t * 128 : t * 128 + 128, :], AR[1], 1, 0)
        D[t // 2, (t % 2) * 2 : (t % 2) * 2 + 2] = acc.reshape(2, 8, 8, 512)
    d_mate = remote(D.at[k], DP, dp_s, dp_r, mate)
    d_mate.start()

    q_steps(1, 2)

    d_mate.wait_recv()

    @pl.loop(0, NY)
    def _(yy):
        D[c, :, yy] += DP[:, yy]

    for d in range(1, NY):
        to = lax.rem(y + d, NY)
        remote(D.at[c, :, to], DY.at[d - 1], dy_s.at[d - 1], dy_r.at[d - 1], dev(x, to, z, c)).start()

    q_steps(2, 5)

    total = D[c, :, y]
    for d in range(1, NY):
        remote(D.at[c, :, 0], DY.at[d - 1], dy_s.at[d - 1], dy_r.at[d - 1], mate).wait_recv()
        total += DY[d - 1]
    for i in range(2):
        DX[0, i] = total[2 * i : 2 * i + 2]
    act = x // 2 == c
    for i in range(2):

        @pl.when(2 * c + i != x)
        def _():
            to = 2 * c + i
            slot = lax.rem(x + NX - to, NX)
            remote(DX.at[0, i], DX.at[slot, 0], dx_s.at[i], dx_r.at[slot], dev(to, y, z, c)).start()

    q_steps(5, 6)

    @pl.when(act)
    def _():
        tot = DX[0, x - 2 * c]
        for slot in range(1, NX):
            remote(DX.at[0, 0], DX.at[slot, 0], dx_s.at[0], dx_r.at[slot], mate).wait_recv()
            tot += DX[slot, 0]
        for t in range(4):
            DZ[:, t] = tot[:, :, t * 128 : t * 128 + 128]
        DR[0] = DZ[h, l // 2]

        for d in range(1, NZ):
            zt = lax.rem(z + d, NZ)
            remote(
                DZ.at[zt // 8, (zt % 8) // 2], DR.at[d], dz_s.at[d], dz_r.at[d], dev(x, y, zt, c)
            ).start()

    q_steps(6, 7)
    for q in range(2):
        mine = own(lax.rem(z + 1, NZ), q)
        q_copy(QR, 6, q, True).wait_recv()
        QR[7, q] += mine
        q_copy(QR, 7, q, True).start()
    for q in range(2):
        mine = own(z, q)
        q_copy(QL, 6, q, False).wait_recv()
        QL[7, q] += mine
    for q in range(2):
        q_copy(QR, 7, q, True).wait_recv()
        got = QR[8, q] + QL[7, q]
        for i in range(16):
            SB[q * 16 + i, 0:BR] = got[i * BR : i * BR + BR]
        for i in range(16):
            b = q * 16 + i

            @pl.when(b != ip)
            def _():
                remote(SB.at[b], R.at[c, ip], a_s.at[b], a_r.at[ip], dev(b // 8, b % 8, z, c)).start()

    R[c, ip] = SB[ip]

    @pl.when(act)
    def _():
        tile = DR[0]
        for d in range(1, NZ):
            remote(DR.at[0], DR.at[d], dz_s.at[d], dz_r.at[d], mate).wait_recv()
            tile += DR[d]
        DO[...] = tile
        remote(DO, DO, do_s, do_r, mate).start()

    @pl.loop(1, PLANE)
    def _(d):
        b = lax.rem(ip + d, PLANE)
        remote(SB.at[b], R.at[c, b], a_s.at[b], a_r.at[b], mate).wait_recv()

    half = remote(R.at[c], R.at[c], r_s, r_r, mate)
    half.start()

    @pl.when(jnp.logical_not(act))
    def _():
        remote(DO, DO, do_s, do_r, mate).wait_recv()

    dens_out[...] = DO[...]

    @pl.when(home)
    def _():
        remote(bs.at[k], S.at[k, x, h, y], w_s.at[0], w_r.at[0], mate).wait_send()

    @pl.when(jnp.logical_not(home))
    def _():
        remote(bf, F.at[ja], f0_s, f0_r, mate).wait_send()
        remote(bs.at[c], S.at[c, x, h, y], w_s.at[0], w_r.at[1], mate).wait_send()
        remote(bs.at[k], S.at[k, x, h, y], w_s.at[1], w_r.at[1], mate).wait_send()

    for right in (True, False):
        ss = fr_s if right else fl_s
        for s in range(8 if right else 7):
            o = lax.rem(z + NZ - s, NZ) if right else lax.rem(z + s, NZ)

            @pl.when(o // 8 == c)
            def _():
                for q in range(2):
                    b = F.at[lax.rem(o, NL) * 2 + q]
                    remote(b, b, ss.at[s, q], fr_r.at[s, q], mate).wait_send()

    for slot in range(2):
        for s in range(4):
            y_copy(h, slot, s, True).wait_send()
            if s < 3:
                y_copy(h, slot, s, False).wait_send()
        for n in range(NY):
            b = y_block(h, 0)
            remote(b, b, pc_s.at[slot, n], pc_r.at[slot, n], mate).wait_send()
    for s in range(8):
        for q in range(2):
            q_copy(QR, s, q, True).wait_send()
            if s < 7:
                q_copy(QL, s, q, False).wait_send()
    d_mate.wait_send()
    for d in range(1, NY):
        remote(D.at[c, :, 0], DY.at[d - 1], dy_s.at[d - 1], dy_r.at[d - 1], mate).wait_send()
    for i in range(2):

        @pl.when(2 * c + i != x)
        def _():
            remote(DX.at[0, i], DX.at[1, 0], dx_s.at[i], dx_r.at[1], mate).wait_send()

    @pl.when(act)
    def _():
        for d in range(1, NZ):
            remote(DR.at[0], DR.at[d], dz_s.at[d], dz_r.at[d], mate).wait_send()
        remote(DO, DO, do_s, do_r, mate).wait_send()

    @pl.loop(1, PLANE)
    def _(d):
        b = lax.rem(ip + d, PLANE)
        remote(SB.at[b], R.at[c, b], a_s.at[b], a_r.at[b], mate).wait_send()

    half.wait_send()
    remote(R.at[k], R.at[k], r_s, r_r, mate).wait_recv()


def last_kernel(r, co, dens, gamma, density, W, L):
    _, _, _, l, c = place()
    W[...] = jnp.zeros_like(W)
    for hi in range(2):
        for x in range(NX):
            rows = co[(x * 2 + hi) * 8 : (x * 2 + hi) * 8 + 8, :]
            at = hi * 32 + x * 8
            W[at : at + 8, 0:576] = rows
            W[64 + at : 64 + at + 8, 576:1152] = rows
    w_hi, w_lo = split(W[...])
    for n in range(BR):
        both = jnp.transpose(r[:, :, n, :].reshape(64, 128))
        L[0, n], L[1, n] = both[0:64], both[64:128]
    for n in range(BR):
        even = L[c, n, pl.ds(0, 32, stride=2), :]
        odd = L[c, n, pl.ds(1, 32, stride=2), :]
        l_hi, l_lo = split(jnp.concatenate([even, odd], axis=1))
        res = dot(l_hi, w_hi, 1, 0) + dot(l_lo, w_hi, 1, 0) + dot(l_hi, w_lo, 1, 0)
        for t in range(32):
            gamma[n : n + 1, t * 1152 : t * 1152 + 1152] = res[t : t + 1, :]
    at = (l % 2) * 64 + c * 32
    turned = pltpu.roll(dens[...], lax.rem(128 - at, 128), 1)
    density[...] = turned[:, 0:32] * (1.0 / 2048.0)


def on_device(b_first, b_second, eps_first, eps_second, eps_virtual, c_virtual, c_occupied):
    bf = jnp.swapaxes(b_first, 1, 2)[0]
    bs = jnp.swapaxes(b_second, 1, 2)
    dma = pltpu.SemaphoreType.DMA
    vm = pl.BlockSpec(memory_space=pltpu.VMEM)
    sm = pl.BlockSpec(memory_space=pltpu.SMEM)
    r, dens = pl.pallas_call(
        main_kernel,
        out_shape=(
            jax.ShapeDtypeStruct((2, PLANE, 16, 128), F32),
            jax.ShapeDtypeStruct((8, 128), F32),
        ),
        in_specs=[vm, vm, sm, sm, vm, vm],
        out_specs=(vm, vm),
        scratch_shapes=[
            pltpu.VMEM((16, 64, 512), BF16),
            pltpu.VMEM((2, NX, NH, NY, 16, 512), BF16),
            pltpu.VMEM((3, 3, 8, 128), F32),
            pltpu.VMEM((8, CR, 512), BF16),
            pltpu.VMEM((8, CR, 512), BF16),
            pltpu.VMEM((2, 512, 512), BF16),
            pltpu.VMEM((2, 512, 512), BF16),
            pltpu.VMEM((8, 512, 128), BF16),
            pltpu.VMEM((8, 512, 128), BF16),
            pltpu.VMEM((2, 4, 8, 8, 512), F32),
            pltpu.VMEM((4, 8, 8, 512), F32),
            pltpu.VMEM((7, 4, 8, 512), F32),
            pltpu.VMEM((4, 2, 2, 8, 512), F32),
            pltpu.VMEM((2, 4, 8, 128), F32),
            pltpu.VMEM((16, 8, 128), F32),
            pltpu.VMEM((8, 128), F32),
            pltpu.VMEM((9, 2, 144, 128), F32),
            pltpu.VMEM((8, 2, 144, 128), F32),
            pltpu.VMEM((PLANE, 16, 128), F32),
            dma, dma, dma((8, 2)), dma((8, 2)), dma((7, 2)), dma((7, 2)),
            dma((2,)), dma((2,)), dma((2, 3)), dma((2, 3)),
            dma((2, 4)), dma((2, 4)), dma((2, 3)), dma((2, 3)), dma((2, 8)), dma((2, 8)),
            dma((2,)), dma((2,)),
            dma((8, 2)), dma((8, 2)), dma((7, 2)), dma((7, 2)), dma, dma, dma((7,)), dma((7,)),
            dma((2,)), dma((4,)), dma((16,)), dma((16,)), dma, dma,
            dma((PLANE,)), dma((PLANE,)), dma, dma, dma((2,)),
        ],
        compiler_params=pltpu.CompilerParams(
            collective_id=0, has_side_effects=True, vmem_limit_bytes=48 << 20
        ),
        name="pairs",
    )(bf, bs, eps_first, eps_second, eps_virtual.reshape(1, 512), c_virtual.reshape(8, CR, 512))
    return pl.pallas_call(
        last_kernel,
        out_shape=(
            jax.ShapeDtypeStruct((BR, 36864), F32),
            jax.ShapeDtypeStruct((8, 32), F32),
        ),
        in_specs=[vm, vm, vm],
        out_specs=(vm, vm),
        scratch_shapes=[pltpu.VMEM((128, 1152), F32), pltpu.VMEM((2, BR, 64, 64), F32)],
        name="last",
    )(r, c_occupied, dens)


def solution(mesh):
    return jax.shard_map(
        on_device,
        mesh=mesh,
        in_specs=(P("ia", None, "ja"), P("ja", None, "ia"), P("ia"), P("ja"), P(), P(), P()),
        out_specs=(P("ia", "ja"), P("ia", "ja")),
        check_vma=False,
    )
```

```python
import jax
import jax.numpy as jnp
from jax import lax
from jax.experimental import pallas as pl
from jax.experimental.pallas import tpu as pltpu
from jax.sharding import PartitionSpec as P

F32, BF16 = jnp.float32, jnp.bfloat16
MESH = pl.DeviceIdType.MESH
NX, NY, NH, NL, NZ = 4, 8, 2, 8, 16
PLANE = NX * NY
CR = 72
BR = 9


def dot(a, b, ca, cb):
    return lax.dot_general(a, b, (((ca,), (cb,)), ((), ())), preferred_element_type=F32)


def split(v):
    hi = v.astype(BF16)
    return hi, (v - hi.astype(F32)).astype(BF16)


def place():
    ia, ja = lax.axis_index("ia"), lax.axis_index("ja")
    return ia // 16, (ia // 8) % 2, ia % 8, ja // 2, ja % 2


def dev(x, y, z, c):
    return ((x * 2 + z // 8) * 8 + y, (z % 8) * 2 + c)


def remote(src, dst, ss, rs, to):
    return pltpu.make_async_remote_copy(
        src_ref=src, dst_ref=dst, send_sem=ss, recv_sem=rs, device_id=to, device_id_type=MESH
    )


def main_kernel(
    bf, bs, e1, e2, ev_hbm, cv_hbm,
    R, dens_out,
    ev, cv,
    F, S, E, Chi, Clo, T, AR, G, D, DP, DY, DX, DZ, DR, DO, QR, QL, SB,
    f0_s, f0_r, fr_s, fr_r, fl_s, fl_r,
    w_s, w_r, xa_s, xa_r, xb_s, xb_r, ya_s, ya_r, yb_s, yb_r, pc_s, pc_r, e_s, e_r,
    qr_s, qr_r, ql_s, ql_r, dp_s, dp_r, dy_s, dy_r, dx_s, dx_r, dz_s, dz_r, do_s, do_r,
    a_s, a_r, r_s, r_r, loc,
):
    x, h, y, l, c = place()
    z = h * 8 + l
    k = 1 - c
    ip = x * 8 + y
    ja = l * 2 + c
    home = c == h
    mate = dev(x, y, z, k)
    far = lax.rem(z + 8, NZ)

    E[0, 0] = jnp.full((8, 128), e1[0], F32)
    E[0, 1] = jnp.full((8, 128), e2[0], F32)
    E[0, 2] = jnp.full((8, 128), e2[1], F32)
    cv_in = pltpu.make_async_copy(cv_hbm, cv, loc.at[2])
    ev_in = pltpu.make_async_copy(ev_hbm, ev, loc.at[3])
    cv_in.start()
    ev_in.start()
    barrier = pltpu.get_barrier_semaphore()

    def hail(to):
        pl.semaphore_signal(barrier, inc=1, device_id=to, device_id_type=MESH)

    hail(mate)
    hail(dev(x, y, far, k))

    @pl.loop(1, NZ)
    def _(d):
        hail(dev(x, y, lax.rem(z + d, NZ), c))

    @pl.loop(1, PLANE)
    def _(d):
        q = lax.rem(ip + d, PLANE)
        hail(dev(q // 8, q % 8, z, c))

    pl.semaphore_wait(barrier, 2 + NZ - 1 + PLANE - 1)

    e_far = remote(E.at[0], E.at[1], e_s.at[0], e_r.at[0], dev(x, y, far, c))
    e_mate = remote(E.at[0], E.at[2], e_s.at[1], e_r.at[1], mate)
    s_own = [S.at[j, x, h, y] for j in range(2)]

    @pl.when(home)
    def _():
        remote(bs.at[k], S.at[k, x, h, y], w_s.at[0], w_r.at[0], mate).start()
        pltpu.make_async_copy(bs.at[c], S.at[c, x, h, y], loc.at[0]).start()
        pltpu.make_async_copy(bf, F.at[ja], loc.at[1]).start()

    @pl.when(jnp.logical_not(home))
    def _():
        remote(bf, F.at[ja], f0_s, f0_r, mate).start()
        remote(bs.at[c], S.at[c, x, h, y], w_s.at[0], w_r.at[1], dev(x, y, far, c)).start()
        remote(bs.at[k], S.at[k, x, h, y], w_s.at[1], w_r.at[1], dev(x, y, far, k)).start()

    e_far.start()
    e_mate.start()

    cv_in.wait()
    ev_in.wait()
    for hd in range(NH):
        for q in range(2):
            v = jnp.concatenate([cv[4 * q + hd], cv[4 * q + 2 + hd]], axis=0)
            Chi[hd, q], Clo[hd, q] = split(v)

    first = c == 0
    ROWS = (4, 3, 5, 2, 6, 1, 7)
    LINES = (2, 1, 3)

    def piece(hp):
        return S.at[c, x, hp, y]

    def line(hp, xo):
        return S.at[c, xo, hp]

    def column(hp, yo):
        return S.at[c, :, hp, yo]

    def along_y(ref, to, slot, d, stage):
        ss, rs = (ya_s, ya_r) if stage == 1 else (yb_s, yb_r)
        return remote(ref, ref, ss.at[slot, d], rs.at[slot, d], dev(x, to, z, c))

    def along_x(ref, to, slot, d, stage):
        ss, rs = (xa_s, xa_r) if stage == 1 else (xb_s, xb_r)
        return remote(ref, ref, ss.at[slot, d], rs.at[slot, d], dev(to, y, z, c))

    def share(ref, slot, n):
        remote(ref, ref, pc_s.at[slot, n], pc_r.at[slot, n], mate).start()

    def stage_1(hp, slot):
        @pl.when(first)
        def _():
            for d in ROWS:
                along_y(piece(hp), lax.rem(y + d, NY), slot, d, 1).start()

        @pl.when(jnp.logical_not(first))
        def _():
            for d in LINES:
                along_x(piece(hp), lax.rem(x + d, NX), slot, d, 1).start()

    def stage_2(hp, slot):
        @pl.when(first)
        def _():
            for d in ROWS:
                along_y(S.at[c, x, hp, lax.rem(y + NY - d, NY)], yr, slot, d, 1).wait_recv()
            for d in LINES:
                along_x(line(hp, x), lax.rem(x + d, NX), slot, d, 2).start()
            share(line(hp, x), slot, 0)

        @pl.when(jnp.logical_not(first))
        def _():
            for d in LINES:
                along_x(S.at[c, lax.rem(x + NX - d, NX), hp, y], lax.rem(x + 1, NX), slot, d, 1).wait_recv()
            for d in ROWS:
                along_y(column(hp, y), lax.rem(y + d, NY), slot, d, 2).start()
            share(column(hp, y), slot, 0)

    def stage_3(hp, slot, lines, rows):
        @pl.when(first)
        def _():
            for d in lines:
                b = line(hp, lax.rem(x + NX - d, NX))
                along_x(b, lax.rem(x + 1, NX), slot, d, 2).wait_recv()
                share(b, slot, d)

        @pl.when(jnp.logical_not(first))
        def _():
            for d in rows:
                b = column(hp, lax.rem(y + NY - d, NY))
                along_y(b, yr, slot, d, 2).wait_recv()
                share(b, slot, d)

    yr = lax.rem(y + 1, NY)

    zr, zl = lax.rem(z + 1, NZ), lax.rem(z + NZ - 1, NZ)

    def f_step(s):
        for right in (True, False):
            last = 8 if right else 7
            if s > last:
                continue
            o = lax.rem(z + NZ - s, NZ) if right else lax.rem(z + s, NZ)
            ss, rs = (fr_s, fr_r) if right else (fl_s, fl_r)
            to = dev(x, y, zr if right else zl, c)

            @pl.when(o // 8 == c)
            def _():
                for q in range(4):
                    b = F.at[lax.rem(o, NL) * 2 + q // 2, pl.ds(q % 2 * 32, 32)]
                    if s > 0:
                        remote(b, b, ss.at[s - 1, q], rs.at[s - 1, q], to).wait_recv()
                    if s < last:
                        remote(b, b, ss.at[s, q], rs.at[s, q], to).start()

    @pl.when(home)
    def _():
        pltpu.make_async_copy(bs.at[c], S.at[c, x, h, y], loc.at[0]).wait()
        pltpu.make_async_copy(bf, F.at[ja], loc.at[1]).wait()
        remote(bf, F.at[l * 2 + k], f0_s, f0_r, mate).wait_recv()

    @pl.when(jnp.logical_not(home))
    def _():
        remote(bs.at[c], S.at[c, x, h, y], w_s.at[0], w_r.at[0], mate).wait_recv()

    other = 1 - h
    stage_1(h, 0)
    f_step(0)
    f_step(1)
    stage_2(h, 0)
    f_step(2)
    remote(bs.at[c], S.at[c, x, other, y], w_s.at[0], w_r.at[1], mate).wait_recv()
    stage_1(other, 1)
    f_step(3)
    f_step(4)
    stage_2(other, 1)
    f_step(5)
    stage_3(h, 0, LINES, ROWS)
    f_step(6)
    f_step(7)
    stage_3(other, 1, LINES[:1], ROWS[:3])
    f_step(8)
    stage_3(other, 1, LINES[1:], ROWS[3:])

    e_far.wait()
    e_mate.wait()
    for slot, hp in ((0, h), (1, other)):

        @pl.when(first)
        def _():
            for n in range(NY):
                b = S.at[k, :, hp, lax.rem(y + NY - n, NY)]
                remote(b, b, pc_s.at[slot, n], pc_r.at[slot, n], mate).wait_recv()

        @pl.when(jnp.logical_not(first))
        def _():
            for n in range(NX):
                b = S.at[k, lax.rem(x + NX - n, NX), hp]
                remote(b, b, pc_s.at[slot, n], pc_r.at[slot, n], mate).wait_recv()

    ei = jnp.where(home, E[0, 0, 0:1, 0:1], E[1, 0, 0:1, 0:1])
    row = ev[...]
    for j in range(2):
        ej = jnp.where(home, E[0, 1 + j, 0:1, 0:1], E[2, 1 + j, 0:1, 0:1])

        @pl.loop(0, 4)
        def _(t):
            cols = pl.ds(pl.multiple_of(t * 128, 128), 128)
            full_s = S[j].reshape(1024, 512)
            full_f = F[...].reshape(1024, 512)
            tile_f = F[:, :, cols].reshape(1024, 128)
            tile_s = S[j, :, :, :, :, cols].reshape(1024, 128)
            i_ab = dot(tile_f, full_s, 0, 0)
            i_ba = dot(tile_s, full_f, 0, 0)
            col = jnp.transpose(jnp.broadcast_to(ev[:, cols], (128, 128)))[:, 0:1]
            r = 1.0 / (ei + ej - (col + row))
            a = i_ab * r
            at = i_ba * r
            rows = pl.ds(pl.multiple_of(t * 128, 128), 128)
            T[j, rows, :] = (2.0 * a - at).astype(BF16)
            AR[j, rows, :] = at.astype(BF16)

    @pl.loop(0, 8)
    def _(g):
        gx, gh = g // 2, g % 2
        acc = dot(T[0], S[0, gx, gh].reshape(128, 512), 1, 1)
        acc += dot(T[1], S[1, gx, gh].reshape(128, 512), 1, 1)
        hi, lo = split(acc)
        G[g, :, 0:128] = hi
        G[g, :, 128:256] = lo

    def own(d):
        hd, ld = d // 8, d % 8
        both = dot(Chi[hd].reshape(288, 512), G[ld], 1, 0)
        out = both[:, 0:128] + both[:, 128:256] + dot(Clo[hd].reshape(288, 512), G[ld, :, 0:128], 1, 0)
        return out[0:144], out[144:288]

    def q_copy(buf, s, q, right):
        ss, rs = (qr_s, qr_r) if right else (ql_s, ql_r)
        return remote(
            buf.at[s, q], buf.at[s + 1, q], ss.at[s, q], rs.at[s, q], dev(x, y, zr if right else zl, c)
        )

    for right, buf in ((True, QR), (False, QL)):
        d0 = lax.rem(z + (8 if right else 9), NZ)
        mine = own(d0)
        for q in range(2):
            buf[0, q] = mine[q]
            q_copy(buf, 0, q, right).start()

    def q_steps(lo, hi):
        @pl.loop(lo, hi)
        def _(s):
            dr = lax.rem(z + 8 + NZ - s, NZ)
            dl = lax.rem(z + 9 + s, NZ)
            for right, buf, d in ((True, QR, dr), (False, QL, dl)):
                mine = own(d)
                for q in range(2):
                    q_copy(buf, s - 1, q, right).wait_recv()
                    buf[s, q] += mine[q]
                    q_copy(buf, s, q, right).start()

    for t in range(4):
        acc = dot(T[0, t * 128 : t * 128 + 128, :], AR[0], 1, 0)
        acc += dot(T[1, t * 128 : t * 128 + 128, :], AR[1], 1, 0)
        D[t // 2, (t % 2) * 2 : (t % 2) * 2 + 2] = acc.reshape(2, 8, 8, 512)
    d_mate = remote(D.at[k], DP, dp_s, dp_r, mate)
    d_mate.start()

    q_steps(1, 2)

    d_mate.wait_recv()

    @pl.loop(0, NY)
    def _(yy):
        D[c, :, yy] += DP[:, yy]

    for d in range(1, NY):
        to = lax.rem(y + d, NY)
        remote(D.at[c, :, to], DY.at[d - 1], dy_s.at[d - 1], dy_r.at[d - 1], dev(x, to, z, c)).start()

    q_steps(2, 5)

    total = D[c, :, y]
    for d in range(1, NY):
        remote(D.at[c, :, 0], DY.at[d - 1], dy_s.at[d - 1], dy_r.at[d - 1], mate).wait_recv()
        total += DY[d - 1]
    for i in range(2):
        DX[0, i] = total[2 * i : 2 * i + 2]
    act = x // 2 == c
    for i in range(2):

        @pl.when(2 * c + i != x)
        def _():
            to = 2 * c + i
            slot = lax.rem(x + NX - to, NX)
            remote(DX.at[0, i], DX.at[slot, 0], dx_s.at[i], dx_r.at[slot], dev(to, y, z, c)).start()

    q_steps(5, 6)

    @pl.when(act)
    def _():
        tot = DX[0, x - 2 * c]
        for slot in range(1, NX):
            remote(DX.at[0, 0], DX.at[slot, 0], dx_s.at[0], dx_r.at[slot], mate).wait_recv()
            tot += DX[slot, 0]
        for t in range(4):
            DZ[:, t] = tot[:, :, t * 128 : t * 128 + 128]
        DR[0] = DZ[h, l // 2]

        for d in range(1, NZ):
            zt = lax.rem(z + d, NZ)
            remote(
                DZ.at[zt // 8, (zt % 8) // 2], DR.at[d], dz_s.at[d], dz_r.at[d], dev(x, y, zt, c)
            ).start()

    q_steps(6, 7)
    mine = own(lax.rem(z + 1, NZ))
    for q in range(2):
        q_copy(QR, 6, q, True).wait_recv()
        QR[7, q] += mine[q]
        q_copy(QR, 7, q, True).start()
    mine = own(z)
    for q in range(2):
        q_copy(QL, 6, q, False).wait_recv()
        QL[7, q] += mine[q]
    for q in range(2):
        q_copy(QR, 7, q, True).wait_recv()
        got = QR[8, q] + QL[7, q]
        for i in range(16):
            SB[q * 16 + i] = got[i * BR : i * BR + BR]
        for i in range(16):
            b = q * 16 + i

            @pl.when(b != ip)
            def _():
                remote(SB.at[b], R.at[c, ip], a_s.at[b], a_r.at[ip], dev(b // 8, b % 8, z, c)).start()

    R[c, ip] = SB[ip]

    @pl.when(act)
    def _():
        tile = DR[0]
        for d in range(1, NZ):
            remote(DR.at[0], DR.at[d], dz_s.at[d], dz_r.at[d], mate).wait_recv()
            tile += DR[d]
        DO[...] = tile
        remote(DO, DO, do_s, do_r, mate).start()

    def group(core, d):
        b = R.at[core, pl.ds(lax.rem(x + d, NX) * NY, NY)]
        return remote(b, b, r_s.at[d], r_r.at[d], mate)

    for d in (0, 1, 3, 2):

        @pl.loop(0, NY)
        def _(yy):
            b = lax.rem(x + d, NX) * NY + yy

            @pl.when(b != ip)
            def _():
                remote(SB.at[b], R.at[c, b], a_s.at[b], a_r.at[b], mate).wait_recv()

        group(c, d).start()

    @pl.when(jnp.logical_not(act))
    def _():
        remote(DO, DO, do_s, do_r, mate).wait_recv()

    dens_out[...] = DO[...]

    @pl.when(home)
    def _():
        remote(bs.at[k], S.at[k, x, h, y], w_s.at[0], w_r.at[0], mate).wait_send()

    @pl.when(jnp.logical_not(home))
    def _():
        remote(bf, F.at[ja], f0_s, f0_r, mate).wait_send()
        remote(bs.at[c], S.at[c, x, h, y], w_s.at[0], w_r.at[1], mate).wait_send()
        remote(bs.at[k], S.at[k, x, h, y], w_s.at[1], w_r.at[1], mate).wait_send()

    for right in (True, False):
        ss = fr_s if right else fl_s
        for s in range(8 if right else 7):
            o = lax.rem(z + NZ - s, NZ) if right else lax.rem(z + s, NZ)

            @pl.when(o // 8 == c)
            def _():
                for q in range(4):
                    b = F.at[lax.rem(o, NL) * 2 + q // 2, pl.ds(q % 2 * 32, 32)]
                    remote(b, b, ss.at[s, q], fr_r.at[s, q], mate).wait_send()

    for slot in range(2):

        @pl.when(first)
        def _():
            for d in ROWS:
                along_y(piece(h), yr, slot, d, 1).wait_send()
            for d in LINES:
                along_x(line(h, x), lax.rem(x + 1, NX), slot, d, 2).wait_send()
            for n in range(NX):
                remote(line(h, x), line(h, x), pc_s.at[slot, n], pc_r.at[slot, n], mate).wait_send()

        @pl.when(jnp.logical_not(first))
        def _():
            for d in LINES:
                along_x(piece(h), lax.rem(x + 1, NX), slot, d, 1).wait_send()
            for d in ROWS:
                along_y(column(h, y), yr, slot, d, 2).wait_send()
            for n in range(NY):
                remote(column(h, y), column(h, y), pc_s.at[slot, n], pc_r.at[slot, n], mate).wait_send()

    for s in range(8):
        for q in range(2):
            q_copy(QR, s, q, True).wait_send()
            if s < 7:
                q_copy(QL, s, q, False).wait_send()
    d_mate.wait_send()
    for d in range(1, NY):
        remote(D.at[c, :, 0], DY.at[d - 1], dy_s.at[d - 1], dy_r.at[d - 1], mate).wait_send()
    for i in range(2):

        @pl.when(2 * c + i != x)
        def _():
            remote(DX.at[0, i], DX.at[1, 0], dx_s.at[i], dx_r.at[1], mate).wait_send()

    @pl.when(act)
    def _():
        for d in range(1, NZ):
            remote(DR.at[0], DR.at[d], dz_s.at[d], dz_r.at[d], mate).wait_send()
        remote(DO, DO, do_s, do_r, mate).wait_send()

    @pl.loop(1, PLANE)
    def _(d):
        b = lax.rem(ip + d, PLANE)
        remote(SB.at[b], R.at[c, b], a_s.at[b], a_r.at[b], mate).wait_send()

    for d in range(NX):
        group(c, d).wait_send()
        group(k, d).wait_recv()


def last_kernel(r, co_hbm, dens, gamma_hbm, density, co, gamma, W, LT, L, sem, out_sem):
    _, _, _, l, c = place()
    co_in = pltpu.make_async_copy(co_hbm, co, sem)
    co_in.start()
    W[...] = jnp.zeros_like(W)
    co_in.wait()
    for hi in range(2):
        for x in range(NX):
            rows = co[(x * 2 + hi) * 8 : (x * 2 + hi) * 8 + 8, :]
            at = hi * 32 + x * 8
            W[at : at + 8, 0:576] = rows
            W[64 + at : 64 + at + 8, 576:1152] = rows
    w_hi, w_lo = split(W[...])
    for n in range(BR):
        LT[n] = jnp.transpose(r[:, :, n, :].reshape(64, 128))
        even = LT[n, pl.ds(c * 64, 32, stride=2), :]
        odd = LT[n, pl.ds(c * 64 + 1, 32, stride=2), :]
        L[pl.ds(n, 32, stride=16), :] = jnp.concatenate([even, odd], axis=1)
    outs = []
    for g in range(4):
        l_hi, l_lo = split(L[g * 128 : g * 128 + 128, :])
        res = dot(l_hi, w_hi, 1, 0) + dot(l_lo, w_hi, 1, 0) + dot(l_hi, w_lo, 1, 0)
        for t in range(8):
            at = (g * 8 + t) * 1152
            gamma[:, at : at + 1152] = res[t * 16 : t * 16 + BR, :]
        cols = pl.ds(g * 9216, 9216)
        outs.append(pltpu.make_async_copy(gamma.at[:, cols], gamma_hbm.at[:, cols], out_sem.at[g]))
        outs[-1].start()
    at = (l % 2) * 64 + c * 32
    turned = pltpu.roll(dens[...], lax.rem(128 - at, 128), 1)
    density[...] = turned[:, 0:32] * (1.0 / 2048.0)
    for copy in outs:
        copy.wait()


def on_device(b_first, b_second, eps_first, eps_second, eps_virtual, c_virtual, c_occupied):
    bf = jnp.swapaxes(b_first, 1, 2)[0]
    bs = jnp.swapaxes(b_second, 1, 2)
    dma = pltpu.SemaphoreType.DMA
    vm = pl.BlockSpec(memory_space=pltpu.VMEM)
    sm = pl.BlockSpec(memory_space=pltpu.SMEM)
    hb = pl.BlockSpec(memory_space=pltpu.HBM)
    r, dens = pl.pallas_call(
        main_kernel,
        out_shape=(
            jax.ShapeDtypeStruct((2, PLANE, BR, 128), F32),
            jax.ShapeDtypeStruct((8, 128), F32),
        ),
        in_specs=[hb, hb, sm, sm, hb, hb],
        out_specs=(vm, vm),
        scratch_shapes=[
            pltpu.VMEM((1, 512), F32),
            pltpu.VMEM((8, CR, 512), F32),
            pltpu.VMEM((16, 64, 512), BF16),
            pltpu.VMEM((2, NX, NH, NY, 16, 512), BF16),
            pltpu.VMEM((3, 3, 8, 128), F32),
            pltpu.VMEM((NH, 2, 144, 512), BF16),
            pltpu.VMEM((NH, 2, 144, 512), BF16),
            pltpu.VMEM((2, 512, 512), BF16),
            pltpu.VMEM((2, 512, 512), BF16),
            pltpu.VMEM((8, 512, 256), BF16),
            pltpu.VMEM((2, 4, 8, 8, 512), F32),
            pltpu.VMEM((4, 8, 8, 512), F32),
            pltpu.VMEM((7, 4, 8, 512), F32),
            pltpu.VMEM((4, 2, 2, 8, 512), F32),
            pltpu.VMEM((2, 4, 8, 128), F32),
            pltpu.VMEM((16, 8, 128), F32),
            pltpu.VMEM((8, 128), F32),
            pltpu.VMEM((9, 2, 144, 128), F32),
            pltpu.VMEM((8, 2, 144, 128), F32),
            pltpu.VMEM((PLANE, BR, 128), F32),
            dma, dma, dma((8, 4)), dma((8, 4)), dma((7, 4)), dma((7, 4)),
            dma((2,)), dma((2,)), dma((2, 4)), dma((2, 4)), dma((2, 4)), dma((2, 4)),
            dma((2, 8)), dma((2, 8)), dma((2, 8)), dma((2, 8)), dma((2, 8)), dma((2, 8)),
            dma((2,)), dma((2,)),
            dma((8, 2)), dma((8, 2)), dma((7, 2)), dma((7, 2)), dma, dma, dma((7,)), dma((7,)),
            dma((2,)), dma((4,)), dma((16,)), dma((16,)), dma, dma,
            dma((PLANE,)), dma((PLANE,)), dma((NX,)), dma((NX,)), dma((4,)),
        ],
        compiler_params=pltpu.CompilerParams(
            collective_id=0, has_side_effects=True, vmem_limit_bytes=66_560_000
        ),
        name="pairs",
    )(bf, bs, eps_first, eps_second, eps_virtual.reshape(1, 512), c_virtual.reshape(8, CR, 512))
    return pl.pallas_call(
        last_kernel,
        out_shape=(
            jax.ShapeDtypeStruct((BR, 36864), F32),
            jax.ShapeDtypeStruct((8, 32), F32),
        ),
        in_specs=[vm, hb, vm],
        out_specs=(hb, vm),
        scratch_shapes=[
            pltpu.VMEM((64, 576), F32),
            pltpu.VMEM((BR, 36864), F32),
            pltpu.VMEM((128, 1152), F32),
            pltpu.VMEM((BR, 128, 64), F32),
            pltpu.VMEM((512, 128), F32),
            dma,
            dma((4,)),
        ],
        compiler_params=pltpu.CompilerParams(vmem_limit_bytes=66_560_000),
        name="last",
    )(r, c_occupied, dens)


def solution(mesh):
    return jax.shard_map(
        on_device,
        mesh=mesh,
        in_specs=(P("ia", None, "ja"), P("ja", None, "ia"), P("ia"), P("ja"), P(), P(), P()),
        out_specs=(P("ia", "ja"), P("ia", "ja")),
        check_vma=False,
    )
```

```python
import jax
import jax.numpy as jnp
from jax import lax
from jax.experimental import pallas as pl
from jax.experimental.pallas import tpu as pltpu
from jax.sharding import PartitionSpec as P

F32, BF16 = jnp.float32, jnp.bfloat16
MESH = pl.DeviceIdType.MESH
NX, NY, NH, NL, NZ = 4, 8, 2, 8, 16
PLANE = NX * NY
CR = 72
BR = 9


def dot(a, b, ca, cb):
    return lax.dot_general(a, b, (((ca,), (cb,)), ((), ())), preferred_element_type=F32)


def split(v):
    hi = v.astype(BF16)
    return hi, (v - hi.astype(F32)).astype(BF16)


def place():
    ia, ja = lax.axis_index("ia"), lax.axis_index("ja")
    return ia // 16, (ia // 8) % 2, ia % 8, ja // 2, ja % 2


def dev(x, y, z, c):
    return ((x * 2 + z // 8) * 8 + y, (z % 8) * 2 + c)


def remote(src, dst, ss, rs, to):
    return pltpu.make_async_remote_copy(
        src_ref=src, dst_ref=dst, send_sem=ss, recv_sem=rs, device_id=to, device_id_type=MESH
    )


def main_kernel(
    bf, bs, e1, e2, ev_hbm, cv_hbm,
    R, dens_out,
    ev, cv,
    F, S, E, Chi, Clo, T, AR, G32, G, D, DP, DY, DX, DZ, DR, DO, QR, QL, SB,
    f0_s, f0_r, fr_s, fr_r, fl_s, fl_r,
    w_s, w_r, xa_s, xa_r, xb_s, xb_r, ya_s, ya_r, yb_s, yb_r, pc_s, pc_r, e_s, e_r,
    qr_s, qr_r, ql_s, ql_r, dp_s, dp_r, dy_s, dy_r, dx_s, dx_r, dz_s, dz_r, do_s, do_r,
    a_s, a_r, r_s, r_r, loc,
):
    x, h, y, l, c = place()
    z = h * 8 + l
    k = 1 - c
    ip = x * 8 + y
    ja = l * 2 + c
    home = c == h
    mate = dev(x, y, z, k)
    far = lax.rem(z + 8, NZ)

    E[0, 0] = jnp.full((8, 128), e1[0], F32)
    E[0, 1] = jnp.full((8, 128), e2[0], F32)
    E[0, 2] = jnp.full((8, 128), e2[1], F32)
    cv_in = pltpu.make_async_copy(cv_hbm, cv, loc.at[2])
    ev_in = pltpu.make_async_copy(ev_hbm, ev, loc.at[3])
    cv_in.start()
    ev_in.start()
    barrier = pltpu.get_barrier_semaphore()

    def hail(to):
        pl.semaphore_signal(barrier, inc=1, device_id=to, device_id_type=MESH)

    hail(mate)
    hail(dev(x, y, far, k))

    @pl.loop(1, NZ)
    def _(d):
        hail(dev(x, y, lax.rem(z + d, NZ), c))

    @pl.loop(1, PLANE)
    def _(d):
        q = lax.rem(ip + d, PLANE)
        hail(dev(q // 8, q % 8, z, c))

    pl.semaphore_wait(barrier, 2 + NZ - 1 + PLANE - 1)

    e_far = remote(E.at[0], E.at[1], e_s.at[0], e_r.at[0], dev(x, y, far, c))
    e_mate = remote(E.at[0], E.at[2], e_s.at[1], e_r.at[1], mate)
    s_own = [S.at[j, x, h, y] for j in range(2)]

    @pl.when(home)
    def _():
        remote(bs.at[k], S.at[k, x, h, y], w_s.at[0], w_r.at[0], mate).start()
        pltpu.make_async_copy(bs.at[c], S.at[c, x, h, y], loc.at[0]).start()
        pltpu.make_async_copy(bf, F.at[ja], loc.at[1]).start()

    @pl.when(jnp.logical_not(home))
    def _():
        remote(bf, F.at[ja], f0_s, f0_r, mate).start()
        remote(bs.at[c], S.at[c, x, h, y], w_s.at[0], w_r.at[1], dev(x, y, far, c)).start()
        remote(bs.at[k], S.at[k, x, h, y], w_s.at[1], w_r.at[1], dev(x, y, far, k)).start()

    e_far.start()
    e_mate.start()

    cv_in.wait()
    ev_in.wait()
    for hd in range(NH):
        for q in range(2):
            v = jnp.concatenate([cv[4 * q + hd], cv[4 * q + 2 + hd]], axis=0)
            Chi[hd, q], Clo[hd, q] = split(v)

    first = c == 0
    ROWS = (4, 3, 5, 2, 6, 1, 7)
    LINES = (2, 1, 3)

    def piece(hp):
        return S.at[c, x, hp, y]

    def line(hp, xo):
        return S.at[c, xo, hp]

    def column(hp, yo):
        return S.at[c, :, hp, yo]

    def along_y(ref, to, slot, d, stage):
        ss, rs = (ya_s, ya_r) if stage == 1 else (yb_s, yb_r)
        return remote(ref, ref, ss.at[slot, d], rs.at[slot, d], dev(x, to, z, c))

    def along_x(ref, to, slot, d, stage):
        ss, rs = (xa_s, xa_r) if stage == 1 else (xb_s, xb_r)
        return remote(ref, ref, ss.at[slot, d], rs.at[slot, d], dev(to, y, z, c))

    def share(ref, slot, n):
        remote(ref, ref, pc_s.at[slot, n], pc_r.at[slot, n], mate).start()

    def stage_1(hp, slot):
        @pl.when(first)
        def _():
            for d in ROWS:
                along_y(piece(hp), lax.rem(y + d, NY), slot, d, 1).start()

        @pl.when(jnp.logical_not(first))
        def _():
            for d in LINES:
                along_x(piece(hp), lax.rem(x + d, NX), slot, d, 1).start()

    def stage_2(hp, slot):
        @pl.when(first)
        def _():
            for d in ROWS:
                along_y(S.at[c, x, hp, lax.rem(y + NY - d, NY)], yr, slot, d, 1).wait_recv()
            for d in LINES:
                along_x(line(hp, x), lax.rem(x + d, NX), slot, d, 2).start()
            share(line(hp, x), slot, 0)

        @pl.when(jnp.logical_not(first))
        def _():
            for d in LINES:
                along_x(S.at[c, lax.rem(x + NX - d, NX), hp, y], lax.rem(x + 1, NX), slot, d, 1).wait_recv()
            for d in ROWS:
                along_y(column(hp, y), lax.rem(y + d, NY), slot, d, 2).start()
            share(column(hp, y), slot, 0)

    def stage_3(hp, slot, lines, rows):
        @pl.when(first)
        def _():
            for d in lines:
                b = line(hp, lax.rem(x + NX - d, NX))
                along_x(b, lax.rem(x + 1, NX), slot, d, 2).wait_recv()
                share(b, slot, d)

        @pl.when(jnp.logical_not(first))
        def _():
            for d in rows:
                b = column(hp, lax.rem(y + NY - d, NY))
                along_y(b, yr, slot, d, 2).wait_recv()
                share(b, slot, d)

    yr = lax.rem(y + 1, NY)

    zr, zl = lax.rem(z + 1, NZ), lax.rem(z + NZ - 1, NZ)

    def f_step(s):
        for right in (True, False):
            last = 8 if right else 7
            if s > last:
                continue
            o = lax.rem(z + NZ - s, NZ) if right else lax.rem(z + s, NZ)
            ss, rs = (fr_s, fr_r) if right else (fl_s, fl_r)
            to = dev(x, y, zr if right else zl, c)

            @pl.when(o // 8 == c)
            def _():
                for q in range(4):
                    b = F.at[lax.rem(o, NL) * 2 + q // 2, pl.ds(q % 2 * 32, 32)]
                    if s > 0:
                        remote(b, b, ss.at[s - 1, q], rs.at[s - 1, q], to).wait_recv()
                    if s < last:
                        remote(b, b, ss.at[s, q], rs.at[s, q], to).start()

    @pl.when(home)
    def _():
        pltpu.make_async_copy(bs.at[c], S.at[c, x, h, y], loc.at[0]).wait()
        pltpu.make_async_copy(bf, F.at[ja], loc.at[1]).wait()
        remote(bf, F.at[l * 2 + k], f0_s, f0_r, mate).wait_recv()

    @pl.when(jnp.logical_not(home))
    def _():
        remote(bs.at[c], S.at[c, x, h, y], w_s.at[0], w_r.at[0], mate).wait_recv()

    other = 1 - h
    stage_1(h, 0)
    f_step(0)
    f_step(1)
    stage_2(h, 0)
    f_step(2)
    remote(bs.at[c], S.at[c, x, other, y], w_s.at[0], w_r.at[1], mate).wait_recv()
    stage_1(other, 1)
    f_step(3)
    f_step(4)
    stage_2(other, 1)
    f_step(5)
    stage_3(h, 0, LINES, ROWS)
    f_step(6)
    f_step(7)
    stage_3(other, 1, LINES[:1], ROWS[:3])
    f_step(8)
    stage_3(other, 1, LINES[1:], ROWS[3:])

    e_far.wait()
    e_mate.wait()
    ei = jnp.where(home, E[0, 0, 0:1, 0:1], E[1, 0, 0:1, 0:1])
    row = ev[...]

    def amplitude(j):
        ej = jnp.where(home, E[0, 1 + j, 0:1, 0:1], E[2, 1 + j, 0:1, 0:1])

        @pl.loop(0, 4)
        def _(t):
            cols = pl.ds(pl.multiple_of(t * 128, 128), 128)
            full_s = S[j].reshape(1024, 512)
            full_f = F[...].reshape(1024, 512)
            tile_f = F[:, :, cols].reshape(1024, 128)
            tile_s = S[j, :, :, :, :, cols].reshape(1024, 128)
            i_ab = dot(tile_f, full_s, 0, 0)
            i_ba = dot(tile_s, full_f, 0, 0)
            col = jnp.transpose(jnp.broadcast_to(ev[:, cols], (128, 128)))[:, 0:1]
            r = 1.0 / (ei + ej - (col + row))
            a = i_ab * r
            at = i_ba * r
            T[j, cols, :] = (2.0 * a - at).astype(BF16)
            AR[j, cols, :] = at.astype(BF16)

    amplitude(c)

    @pl.loop(0, 8)
    def _(g):
        G32[g] = dot(T[c], S[c, g // 2, g % 2].reshape(128, 512), 1, 1)

    for t in range(4):
        acc = dot(T[c, t * 128 : t * 128 + 128, :], AR[c], 1, 0)
        D[t // 2, (t % 2) * 2 : (t % 2) * 2 + 2] = acc.reshape(2, 8, 8, 512)

    for slot, hp in ((0, h), (1, other)):

        @pl.when(first)
        def _():
            for n in range(NY):
                b = S.at[k, :, hp, lax.rem(y + NY - n, NY)]
                remote(b, b, pc_s.at[slot, n], pc_r.at[slot, n], mate).wait_recv()

        @pl.when(jnp.logical_not(first))
        def _():
            for n in range(NX):
                b = S.at[k, lax.rem(x + NX - n, NX), hp]
                remote(b, b, pc_s.at[slot, n], pc_r.at[slot, n], mate).wait_recv()

    amplitude(k)

    @pl.loop(0, 8)
    def _(g):
        hi, lo = split(G32[g] + dot(T[k], S[k, g // 2, g % 2].reshape(128, 512), 1, 1))
        G[g, :, 0:128] = hi
        G[g, :, 128:256] = lo

    def own(d):
        hd, ld = d // 8, d % 8
        both = dot(Chi[hd].reshape(288, 512), G[ld], 1, 0)
        out = both[:, 0:128] + both[:, 128:256] + dot(Clo[hd].reshape(288, 512), G[ld, :, 0:128], 1, 0)
        return [out[q * CR : q * CR + CR] for q in range(4)]

    def q_copy(buf, s, q, right):
        ss, rs = (qr_s, qr_r) if right else (ql_s, ql_r)
        return remote(
            buf.at[s, q], buf.at[s + 1, q], ss.at[s, q], rs.at[s, q], dev(x, y, zr if right else zl, c)
        )

    EARLY = {True: (0, 1), False: (2, 3)}
    LATE = {True: (2, 3), False: (0, 1)}
    mine = own(lax.rem(z + 8, NZ))
    for right, buf in ((True, QR), (False, QL)):
        for q in EARLY[right]:
            buf[0, q] = mine[q]
            q_copy(buf, 0, q, right).start()
    for right, buf in ((True, QR), (False, QL)):
        mine = own(lax.rem(z + (7 if right else 9), NZ))
        for q in LATE[right]:
            buf[1, q] = mine[q]
            q_copy(buf, 1, q, right).start()
        for q in EARLY[right]:
            q_copy(buf, 0, q, right).wait_recv()
            buf[1, q] += mine[q]
            q_copy(buf, 1, q, right).start()

    def q_steps(lo, hi):
        @pl.loop(lo, hi)
        def _(s):
            dr = lax.rem(z + 8 + NZ - s, NZ)
            dl = lax.rem(z + 8 + s, NZ)
            for right, buf, d in ((True, QR, dr), (False, QL, dl)):
                mine = own(d)
                for q in (*EARLY[right], *LATE[right]):
                    q_copy(buf, s - 1, q, right).wait_recv()
                    buf[s, q] += mine[q]
                    q_copy(buf, s, q, right).start()

    for t in range(4):
        acc = dot(T[k, t * 128 : t * 128 + 128, :], AR[k], 1, 0)
        D[t // 2, (t % 2) * 2 : (t % 2) * 2 + 2] += acc.reshape(2, 8, 8, 512)
    d_mate = remote(D.at[k], DP, dp_s, dp_r, mate)
    d_mate.start()

    q_steps(2, 3)

    d_mate.wait_recv()

    @pl.loop(0, NY)
    def _(yy):
        D[c, :, yy] += DP[:, yy]

    for d in range(1, NY):
        to = lax.rem(y + d, NY)
        remote(D.at[c, :, to], DY.at[d - 1], dy_s.at[d - 1], dy_r.at[d - 1], dev(x, to, z, c)).start()

    q_steps(3, 6)

    total = D[c, :, y]
    for d in range(1, NY):
        remote(D.at[c, :, 0], DY.at[d - 1], dy_s.at[d - 1], dy_r.at[d - 1], mate).wait_recv()
        total += DY[d - 1]
    for i in range(2):
        DX[0, i] = total[2 * i : 2 * i + 2]
    act = x // 2 == c
    for i in range(2):

        @pl.when(2 * c + i != x)
        def _():
            to = 2 * c + i
            slot = lax.rem(x + NX - to, NX)
            remote(DX.at[0, i], DX.at[slot, 0], dx_s.at[i], dx_r.at[slot], dev(to, y, z, c)).start()

    q_steps(6, 7)

    @pl.when(act)
    def _():
        tot = DX[0, x - 2 * c]
        for slot in range(1, NX):
            remote(DX.at[0, 0], DX.at[slot, 0], dx_s.at[0], dx_r.at[slot], mate).wait_recv()
            tot += DX[slot, 0]
        for t in range(4):
            DZ[:, t] = tot[:, :, t * 128 : t * 128 + 128]
        DR[0] = DZ[h, l // 2]

        for d in range(1, NZ):
            zt = lax.rem(z + d, NZ)
            remote(
                DZ.at[zt // 8, (zt % 8) // 2], DR.at[d], dz_s.at[d], dz_r.at[d], dev(x, y, zt, c)
            ).start()

    q_steps(7, 8)
    mine = own(z)
    for q in range(4):
        q_copy(QR, 7, q, True).wait_recv()
        q_copy(QL, 7, q, False).wait_recv()
        got = QR[8, q] + QL[8, q] + mine[q]
        for i in range(NY):
            SB[q * NY + i] = got[i * BR : i * BR + BR]
        for i in range(NY):
            b = q * NY + i

            @pl.when(b != ip)
            def _():
                remote(SB.at[b], R.at[c, ip], a_s.at[b], a_r.at[ip], dev(b // 8, b % 8, z, c)).start()

    R[c, ip] = SB[ip]

    @pl.when(act)
    def _():
        tile = DR[0]
        for d in range(1, NZ):
            remote(DR.at[0], DR.at[d], dz_s.at[d], dz_r.at[d], mate).wait_recv()
            tile += DR[d]
        DO[...] = tile
        remote(DO, DO, do_s, do_r, mate).start()

    def group(core, d):
        b = R.at[core, pl.ds(lax.rem(x + d, NX) * NY, NY)]
        return remote(b, b, r_s.at[d], r_r.at[d], mate)

    for d in (0, 1, 3, 2):

        @pl.loop(0, NY)
        def _(yy):
            b = lax.rem(x + d, NX) * NY + yy

            @pl.when(b != ip)
            def _():
                remote(SB.at[b], R.at[c, b], a_s.at[b], a_r.at[b], mate).wait_recv()

        group(c, d).start()

    @pl.when(jnp.logical_not(act))
    def _():
        remote(DO, DO, do_s, do_r, mate).wait_recv()

    dens_out[...] = DO[...]

    @pl.when(home)
    def _():
        remote(bs.at[k], S.at[k, x, h, y], w_s.at[0], w_r.at[0], mate).wait_send()

    @pl.when(jnp.logical_not(home))
    def _():
        remote(bf, F.at[ja], f0_s, f0_r, mate).wait_send()
        remote(bs.at[c], S.at[c, x, h, y], w_s.at[0], w_r.at[1], mate).wait_send()
        remote(bs.at[k], S.at[k, x, h, y], w_s.at[1], w_r.at[1], mate).wait_send()

    for right in (True, False):
        ss = fr_s if right else fl_s
        for s in range(8 if right else 7):
            o = lax.rem(z + NZ - s, NZ) if right else lax.rem(z + s, NZ)

            @pl.when(o // 8 == c)
            def _():
                for q in range(4):
                    b = F.at[lax.rem(o, NL) * 2 + q // 2, pl.ds(q % 2 * 32, 32)]
                    remote(b, b, ss.at[s, q], fr_r.at[s, q], mate).wait_send()

    for slot in range(2):

        @pl.when(first)
        def _():
            for d in ROWS:
                along_y(piece(h), yr, slot, d, 1).wait_send()
            for d in LINES:
                along_x(line(h, x), lax.rem(x + 1, NX), slot, d, 2).wait_send()
            for n in range(NX):
                remote(line(h, x), line(h, x), pc_s.at[slot, n], pc_r.at[slot, n], mate).wait_send()

        @pl.when(jnp.logical_not(first))
        def _():
            for d in LINES:
                along_x(piece(h), lax.rem(x + 1, NX), slot, d, 1).wait_send()
            for d in ROWS:
                along_y(column(h, y), yr, slot, d, 2).wait_send()
            for n in range(NY):
                remote(column(h, y), column(h, y), pc_s.at[slot, n], pc_r.at[slot, n], mate).wait_send()

    for right, buf in ((True, QR), (False, QL)):
        for s in range(8):
            for q in EARLY[right] if s == 0 else range(4):
                q_copy(buf, s, q, right).wait_send()
    d_mate.wait_send()
    for d in range(1, NY):
        remote(D.at[c, :, 0], DY.at[d - 1], dy_s.at[d - 1], dy_r.at[d - 1], mate).wait_send()
    for i in range(2):

        @pl.when(2 * c + i != x)
        def _():
            remote(DX.at[0, i], DX.at[1, 0], dx_s.at[i], dx_r.at[1], mate).wait_send()

    @pl.when(act)
    def _():
        for d in range(1, NZ):
            remote(DR.at[0], DR.at[d], dz_s.at[d], dz_r.at[d], mate).wait_send()
        remote(DO, DO, do_s, do_r, mate).wait_send()

    @pl.loop(1, PLANE)
    def _(d):
        b = lax.rem(ip + d, PLANE)
        remote(SB.at[b], R.at[c, b], a_s.at[b], a_r.at[b], mate).wait_send()

    for d in range(NX):
        group(c, d).wait_send()
        group(k, d).wait_recv()


def last_kernel(r_hbm, co_hbm, dens, gamma_hbm, density, r, co, gamma, W, LT, L, sem, out_sem):
    _, _, _, l, c = place()
    co_in = pltpu.make_async_copy(co_hbm, co, sem.at[0])
    r_in = pltpu.make_async_copy(r_hbm, r, sem.at[1])
    co_in.start()
    r_in.start()
    W[...] = jnp.zeros_like(W)
    co_in.wait()
    for hi in range(2):
        for x in range(NX):
            rows = co[(x * 2 + hi) * 8 : (x * 2 + hi) * 8 + 8, :]
            at = hi * 32 + x * 8
            W[at : at + 8, 0:576] = rows
            W[64 + at : 64 + at + 8, 576:1152] = rows
    w_hi, w_lo = split(W[...])
    r_in.wait()
    for n in range(BR):
        LT[n] = jnp.transpose(r[:, :, n, :].reshape(64, 128))
        even = LT[n, pl.ds(c * 64, 32, stride=2), :]
        odd = LT[n, pl.ds(c * 64 + 1, 32, stride=2), :]
        L[pl.ds(n, 32, stride=16), :] = jnp.concatenate([even, odd], axis=1)
    outs = []
    for g in range(4):
        l_hi, l_lo = split(L[g * 128 : g * 128 + 128, :])
        res = dot(l_hi, w_hi, 1, 0) + dot(l_lo, w_hi, 1, 0) + dot(l_hi, w_lo, 1, 0)
        for t in range(8):
            at = (g * 8 + t) * 1152
            gamma[:, at : at + 1152] = res[t * 16 : t * 16 + BR, :]
        cols = pl.ds(g * 9216, 9216)
        outs.append(pltpu.make_async_copy(gamma.at[:, cols], gamma_hbm.at[:, cols], out_sem.at[g]))
        outs[-1].start()
    at = (l % 2) * 64 + c * 32
    turned = pltpu.roll(dens[...], lax.rem(128 - at, 128), 1)
    density[...] = turned[:, 0:32] * (1.0 / 2048.0)
    for copy in outs:
        copy.wait()


def on_device(b_first, b_second, eps_first, eps_second, eps_virtual, c_virtual, c_occupied):
    bf = jnp.swapaxes(b_first, 1, 2)[0]
    bs = jnp.swapaxes(b_second, 1, 2)
    dma = pltpu.SemaphoreType.DMA
    vm = pl.BlockSpec(memory_space=pltpu.VMEM)
    sm = pl.BlockSpec(memory_space=pltpu.SMEM)
    hb = pl.BlockSpec(memory_space=pltpu.HBM)
    r, dens = pl.pallas_call(
        main_kernel,
        out_shape=(
            jax.ShapeDtypeStruct((2, PLANE, BR, 128), F32),
            jax.ShapeDtypeStruct((8, 128), F32),
        ),
        in_specs=[hb, hb, sm, sm, hb, hb],
        out_specs=(vm, vm),
        scratch_shapes=[
            pltpu.VMEM((1, 512), F32),
            pltpu.VMEM((8, CR, 512), F32),
            pltpu.VMEM((16, 64, 512), BF16),
            pltpu.VMEM((2, NX, NH, NY, 16, 512), BF16),
            pltpu.VMEM((3, 3, 8, 128), F32),
            pltpu.VMEM((NH, 2, 144, 512), BF16),
            pltpu.VMEM((NH, 2, 144, 512), BF16),
            pltpu.VMEM((2, 512, 512), BF16),
            pltpu.VMEM((2, 512, 512), BF16),
            pltpu.VMEM((8, 512, 128), F32),
            pltpu.VMEM((8, 512, 256), BF16),
            pltpu.VMEM((2, 4, 8, 8, 512), F32),
            pltpu.VMEM((4, 8, 8, 512), F32),
            pltpu.VMEM((7, 4, 8, 512), F32),
            pltpu.VMEM((4, 2, 2, 8, 512), F32),
            pltpu.VMEM((2, 4, 8, 128), F32),
            pltpu.VMEM((16, 8, 128), F32),
            pltpu.VMEM((8, 128), F32),
            pltpu.VMEM((9, 4, CR, 128), F32),
            pltpu.VMEM((9, 4, CR, 128), F32),
            pltpu.VMEM((PLANE, BR, 128), F32),
            dma, dma, dma((8, 4)), dma((8, 4)), dma((7, 4)), dma((7, 4)),
            dma((2,)), dma((2,)), dma((2, 4)), dma((2, 4)), dma((2, 4)), dma((2, 4)),
            dma((2, 8)), dma((2, 8)), dma((2, 8)), dma((2, 8)), dma((2, 8)), dma((2, 8)),
            dma((2,)), dma((2,)),
            dma((8, 4)), dma((8, 4)), dma((8, 4)), dma((8, 4)), dma, dma, dma((7,)), dma((7,)),
            dma((2,)), dma((4,)), dma((16,)), dma((16,)), dma, dma,
            dma((PLANE,)), dma((PLANE,)), dma((NX,)), dma((NX,)), dma((4,)),
        ],
        compiler_params=pltpu.CompilerParams(
            collective_id=0, has_side_effects=True, vmem_limit_bytes=66_560_000
        ),
        name="pairs",
    )(bf, bs, eps_first, eps_second, eps_virtual.reshape(1, 512), c_virtual.reshape(8, CR, 512))
    return pl.pallas_call(
        last_kernel,
        out_shape=(
            jax.ShapeDtypeStruct((BR, 36864), F32),
            jax.ShapeDtypeStruct((8, 32), F32),
        ),
        in_specs=[hb, hb, vm],
        out_specs=(hb, vm),
        scratch_shapes=[
            pltpu.VMEM((2, PLANE, BR, 128), F32),
            pltpu.VMEM((64, 576), F32),
            pltpu.VMEM((BR, 36864), F32),
            pltpu.VMEM((128, 1152), F32),
            pltpu.VMEM((BR, 128, 64), F32),
            pltpu.VMEM((512, 128), F32),
            dma((2,)),
            dma((4,)),
        ],
        compiler_params=pltpu.CompilerParams(vmem_limit_bytes=66_560_000),
        name="last",
    )(r, c_occupied, dens)


def solution(mesh):
    return jax.shard_map(
        on_device,
        mesh=mesh,
        in_specs=(P("ia", None, "ja"), P("ja", None, "ia"), P("ia"), P("ja"), P(), P(), P()),
        out_specs=(P("ia", "ja"), P("ia", "ja")),
        check_vma=False,
    )
```

```python
import jax
import jax.numpy as jnp
from jax import lax
from jax.experimental import pallas as pl
from jax.experimental.pallas import tpu as pltpu
from jax.sharding import PartitionSpec as P

F32, BF16 = jnp.float32, jnp.bfloat16
MESH = pl.DeviceIdType.MESH
NX, NY, NH, NL, NZ = 4, 8, 2, 8, 16
PLANE = NX * NY
CR = 72
BR = 9


def dot(a, b, ca, cb):
    return lax.dot_general(a, b, (((ca,), (cb,)), ((), ())), preferred_element_type=F32)


def split(v):
    hi = v.astype(BF16)
    return hi, (v - hi.astype(F32)).astype(BF16)


def place():
    ia, ja = lax.axis_index("ia"), lax.axis_index("ja")
    return ia // 16, (ia // 8) % 2, ia % 8, ja // 2, ja % 2


def dev(x, y, z, c):
    return ((x * 2 + z // 8) * 8 + y, (z % 8) * 2 + c)


def remote(src, dst, ss, rs, to):
    return pltpu.make_async_remote_copy(
        src_ref=src, dst_ref=dst, send_sem=ss, recv_sem=rs, device_id=to, device_id_type=MESH
    )


def main_kernel(
    bf, bs, e1, e2, ev_hbm, cv_hbm,
    R, dens_out,
    ev, cv,
    F, S, E, Chi, Clo, T, AR, G32, G, D, DP, DY, DX, DZ, DR, DO, QR, QL, SB,
    f0_s, f0_r, fr_s, fr_r, fl_s, fl_r,
    w_s, w_r, xa_s, xa_r, xb_s, xb_r, ya_s, ya_r, yb_s, yb_r, pc_s, pc_r, e_s, e_r,
    qr_s, qr_r, ql_s, ql_r, dp_s, dp_r, dy_s, dy_r, dx_s, dx_r, dz_s, dz_r, do_s, do_r,
    a_s, a_r, r_s, r_r, loc,
):
    x, h, y, l, c = place()
    z = h * 8 + l
    k = 1 - c
    ip = x * 8 + y
    ja = l * 2 + c
    home = c == h
    mate = dev(x, y, z, k)
    far = lax.rem(z + 8, NZ)

    E[0, 0] = jnp.full((8, 128), e1[0], F32)
    E[0, 1] = jnp.full((8, 128), e2[0], F32)
    E[0, 2] = jnp.full((8, 128), e2[1], F32)
    cv_in = pltpu.make_async_copy(cv_hbm, cv, loc.at[2])
    ev_in = pltpu.make_async_copy(ev_hbm, ev, loc.at[3])
    cv_in.start()
    ev_in.start()
    barrier = pltpu.get_barrier_semaphore()

    def hail(to):
        pl.semaphore_signal(barrier, inc=1, device_id=to, device_id_type=MESH)

    hail(mate)
    hail(dev(x, y, far, k))

    @pl.loop(1, NZ)
    def _(d):
        hail(dev(x, y, lax.rem(z + d, NZ), c))

    @pl.loop(1, PLANE)
    def _(d):
        q = lax.rem(ip + d, PLANE)
        hail(dev(q // 8, q % 8, z, c))

    pl.semaphore_wait(barrier, 2 + NZ - 1 + PLANE - 1)

    e_far = remote(E.at[0], E.at[1], e_s.at[0], e_r.at[0], dev(x, y, far, c))
    e_mate = remote(E.at[0], E.at[2], e_s.at[1], e_r.at[1], mate)
    s_own = [S.at[j, x, h, y] for j in range(2)]

    @pl.when(home)
    def _():
        remote(bs.at[k], S.at[k, x, h, y], w_s.at[0], w_r.at[0], mate).start()
        pltpu.make_async_copy(bs.at[c], S.at[c, x, h, y], loc.at[0]).start()
        pltpu.make_async_copy(bf, F.at[ja], loc.at[1]).start()

    @pl.when(jnp.logical_not(home))
    def _():
        remote(bf, F.at[ja], f0_s, f0_r, mate).start()
        remote(bs.at[c], S.at[c, x, h, y], w_s.at[0], w_r.at[1], dev(x, y, far, c)).start()
        remote(bs.at[k], S.at[k, x, h, y], w_s.at[1], w_r.at[1], dev(x, y, far, k)).start()

    e_far.start()
    e_mate.start()

    cv_in.wait()
    ev_in.wait()
    for hd in range(NH):
        for q in range(2):
            v = jnp.concatenate([cv[4 * q + hd], cv[4 * q + 2 + hd]], axis=0)
            Chi[hd, q], Clo[hd, q] = split(v)

    first = c == 0
    ROWS = (4, 3, 5, 2, 6, 1, 7)
    LINES = (2, 1, 3)

    def piece(hp):
        return S.at[c, x, hp, y]

    def line(hp, xo):
        return S.at[c, xo, hp]

    def column(hp, yo):
        return S.at[c, :, hp, yo]

    def along_y(ref, to, slot, d, stage):
        ss, rs = (ya_s, ya_r) if stage == 1 else (yb_s, yb_r)
        return remote(ref, ref, ss.at[slot, d], rs.at[slot, d], dev(x, to, z, c))

    def along_x(ref, to, slot, d, stage):
        ss, rs = (xa_s, xa_r) if stage == 1 else (xb_s, xb_r)
        return remote(ref, ref, ss.at[slot, d], rs.at[slot, d], dev(to, y, z, c))

    def share(ref, slot, n):
        remote(ref, ref, pc_s.at[slot, n], pc_r.at[slot, n], mate).start()

    def stage_1(hp, slot):
        @pl.when(first)
        def _():
            for d in ROWS:
                along_y(piece(hp), lax.rem(y + d, NY), slot, d, 1).start()

        @pl.when(jnp.logical_not(first))
        def _():
            for d in LINES:
                along_x(piece(hp), lax.rem(x + d, NX), slot, d, 1).start()

    def stage_2(hp, slot):
        @pl.when(first)
        def _():
            for d in ROWS:
                along_y(S.at[c, x, hp, lax.rem(y + NY - d, NY)], yr, slot, d, 1).wait_recv()
            for d in LINES:
                along_x(line(hp, x), lax.rem(x + d, NX), slot, d, 2).start()
            share(line(hp, x), slot, 0)

        @pl.when(jnp.logical_not(first))
        def _():
            for d in LINES:
                along_x(S.at[c, lax.rem(x + NX - d, NX), hp, y], lax.rem(x + 1, NX), slot, d, 1).wait_recv()
            for d in ROWS:
                along_y(column(hp, y), lax.rem(y + d, NY), slot, d, 2).start()
            share(column(hp, y), slot, 0)

    def stage_3(hp, slot, lines, rows):
        @pl.when(first)
        def _():
            for d in lines:
                b = line(hp, lax.rem(x + NX - d, NX))
                along_x(b, lax.rem(x + 1, NX), slot, d, 2).wait_recv()
                share(b, slot, d)

        @pl.when(jnp.logical_not(first))
        def _():
            for d in rows:
                b = column(hp, lax.rem(y + NY - d, NY))
                along_y(b, yr, slot, d, 2).wait_recv()
                share(b, slot, d)

    yr = lax.rem(y + 1, NY)

    zr, zl = lax.rem(z + 1, NZ), lax.rem(z + NZ - 1, NZ)

    def f_step(s):
        for right in (True, False):
            last = 8 if right else 7
            if s > last:
                continue
            o = lax.rem(z + NZ - s, NZ) if right else lax.rem(z + s, NZ)
            ss, rs = (fr_s, fr_r) if right else (fl_s, fl_r)
            to = dev(x, y, zr if right else zl, c)

            @pl.when(o // 8 == c)
            def _():
                for q in range(4):
                    b = F.at[lax.rem(o, NL) * 2 + q // 2, pl.ds(q % 2 * 32, 32)]
                    if s > 0:
                        remote(b, b, ss.at[s - 1, q], rs.at[s - 1, q], to).wait_recv()
                    if s < last:
                        remote(b, b, ss.at[s, q], rs.at[s, q], to).start()

    @pl.when(home)
    def _():
        pltpu.make_async_copy(bs.at[c], S.at[c, x, h, y], loc.at[0]).wait()
        pltpu.make_async_copy(bf, F.at[ja], loc.at[1]).wait()
        remote(bf, F.at[l * 2 + k], f0_s, f0_r, mate).wait_recv()

    @pl.when(jnp.logical_not(home))
    def _():
        remote(bs.at[c], S.at[c, x, h, y], w_s.at[0], w_r.at[0], mate).wait_recv()

    other = 1 - h
    stage_1(h, 0)
    f_step(0)
    f_step(1)
    stage_2(h, 0)
    f_step(2)
    remote(bs.at[c], S.at[c, x, other, y], w_s.at[0], w_r.at[1], mate).wait_recv()
    stage_1(other, 1)
    f_step(3)
    f_step(4)
    stage_2(other, 1)
    f_step(5)
    stage_3(h, 0, LINES, ROWS)
    f_step(6)
    f_step(7)
    stage_3(other, 1, LINES[:1], ROWS[:3])
    f_step(8)
    stage_3(other, 1, LINES[1:], ROWS[3:])

    e_far.wait()
    e_mate.wait()
    ei = jnp.where(home, E[0, 0, 0:1, 0:1], E[1, 0, 0:1, 0:1])
    row = ev[...]

    def amplitude(j):
        ej = jnp.where(home, E[0, 1 + j, 0:1, 0:1], E[2, 1 + j, 0:1, 0:1])

        @pl.loop(0, 4)
        def _(t):
            cols = pl.ds(pl.multiple_of(t * 128, 128), 128)
            full_s = S[j].reshape(1024, 512)
            full_f = F[...].reshape(1024, 512)
            tile_f = F[:, :, cols].reshape(1024, 128)
            tile_s = S[j, :, :, :, :, cols].reshape(1024, 128)
            i_ab = dot(tile_f, full_s, 0, 0)
            i_ba = dot(tile_s, full_f, 0, 0)
            col = jnp.transpose(jnp.broadcast_to(ev[:, cols], (128, 128)))[:, 0:1]
            r = 1.0 / (ei + ej - (col + row))
            a = i_ab * r
            at = i_ba * r
            T[j, cols, :] = (2.0 * a - at).astype(BF16)
            AR[j, cols, :] = at.astype(BF16)

    amplitude(c)

    @pl.loop(0, 8)
    def _(g):
        G32[g] = dot(T[c], S[c, g // 2, g % 2].reshape(128, 512), 1, 1)

    for t in range(4):
        acc = dot(T[c, t * 128 : t * 128 + 128, :], AR[c], 1, 0)
        D[t // 2, (t % 2) * 2 : (t % 2) * 2 + 2] = acc.reshape(2, 8, 8, 512)

    for slot, hp in ((0, h), (1, other)):

        @pl.when(first)
        def _():
            for n in range(NY):
                b = S.at[k, :, hp, lax.rem(y + NY - n, NY)]
                remote(b, b, pc_s.at[slot, n], pc_r.at[slot, n], mate).wait_recv()

        @pl.when(jnp.logical_not(first))
        def _():
            for n in range(NX):
                b = S.at[k, lax.rem(x + NX - n, NX), hp]
                remote(b, b, pc_s.at[slot, n], pc_r.at[slot, n], mate).wait_recv()

    amplitude(k)

    @pl.loop(0, 8)
    def _(g):
        hi, lo = split(G32[g] + dot(T[k], S[k, g // 2, g % 2].reshape(128, 512), 1, 1))
        G[g, :, 0:128] = hi
        G[g, :, 128:256] = lo

    def own(d):
        hd, ld = d // 8, d % 8
        both = dot(Chi[hd].reshape(288, 512), G[ld], 1, 0)
        out = both[:, 0:128] + both[:, 128:256] + dot(Clo[hd].reshape(288, 512), G[ld, :, 0:128], 1, 0)
        return [out[q * CR : q * CR + CR] for q in range(4)]

    def q_copy(buf, s, q, right):
        ss, rs = (qr_s, qr_r) if right else (ql_s, ql_r)
        return remote(
            buf.at[s, q], buf.at[s + 1, q], ss.at[s, q], rs.at[s, q], dev(x, y, zr if right else zl, c)
        )

    EARLY = {True: (0, 1), False: (2, 3)}
    LATE = {True: (2, 3), False: (0, 1)}
    mine = own(lax.rem(z + 8, NZ))
    for right, buf in ((True, QR), (False, QL)):
        for q in EARLY[right]:
            buf[0, q] = mine[q]
            q_copy(buf, 0, q, right).start()
    BUF = {True: QR, False: QL}
    LAST = [(right, LATE[right][i]) for i in range(2) for right in (True, False)]
    LEAD = [(right, EARLY[right][i]) for i in range(2) for right in (True, False)]
    mine = {True: own(lax.rem(z + 7, NZ)), False: own(lax.rem(z + 9, NZ))}
    for right, q in LAST:
        BUF[right][1, q] = mine[right][q]
        q_copy(BUF[right], 1, q, right).start()
    for right, q in LEAD:
        q_copy(BUF[right], 0, q, right).wait_recv()
        BUF[right][1, q] += mine[right][q]
        q_copy(BUF[right], 1, q, right).start()

    def q_steps(lo, hi):
        @pl.loop(lo, hi)
        def _(s):
            dr = lax.rem(z + 8 + NZ - s, NZ)
            dl = lax.rem(z + 8 + s, NZ)
            mine = {True: own(dr), False: own(dl)}
            for right, q in (*LAST, *LEAD):
                buf = BUF[right]
                q_copy(buf, s - 1, q, right).wait_recv()
                buf[s, q] += mine[right][q]
                q_copy(buf, s, q, right).start()

    for t in range(4):
        acc = dot(T[k, t * 128 : t * 128 + 128, :], AR[k], 1, 0)
        D[t // 2, (t % 2) * 2 : (t % 2) * 2 + 2] += acc.reshape(2, 8, 8, 512)
    d_mate = remote(D.at[k], DP, dp_s, dp_r, mate)
    d_mate.start()

    q_steps(2, 3)

    d_mate.wait_recv()

    @pl.loop(0, NY)
    def _(yy):
        D[c, :, yy] += DP[:, yy]

    for d in range(1, NY):
        to = lax.rem(y + d, NY)
        remote(D.at[c, :, to], DY.at[d - 1], dy_s.at[d - 1], dy_r.at[d - 1], dev(x, to, z, c)).start()

    q_steps(3, 6)

    total = D[c, :, y]
    for d in range(1, NY):
        remote(D.at[c, :, 0], DY.at[d - 1], dy_s.at[d - 1], dy_r.at[d - 1], mate).wait_recv()
        total += DY[d - 1]
    for i in range(2):
        DX[0, i] = total[2 * i : 2 * i + 2]
    act = x // 2 == c
    for i in range(2):

        @pl.when(2 * c + i != x)
        def _():
            to = 2 * c + i
            slot = lax.rem(x + NX - to, NX)
            remote(DX.at[0, i], DX.at[slot, 0], dx_s.at[i], dx_r.at[slot], dev(to, y, z, c)).start()

    q_steps(6, 7)

    @pl.when(act)
    def _():
        tot = DX[0, x - 2 * c]
        for slot in range(1, NX):
            remote(DX.at[0, 0], DX.at[slot, 0], dx_s.at[0], dx_r.at[slot], mate).wait_recv()
            tot += DX[slot, 0]
        for t in range(4):
            DZ[:, t] = tot[:, :, t * 128 : t * 128 + 128]
        DR[0] = DZ[h, l // 2]

        for d in range(1, NZ):
            zt = lax.rem(z + d, NZ)
            remote(
                DZ.at[zt // 8, (zt % 8) // 2], DR.at[d], dz_s.at[d], dz_r.at[d], dev(x, y, zt, c)
            ).start()

    q_steps(7, 8)
    mine = own(z)
    for q in range(4):
        q_copy(QR, 7, q, True).wait_recv()
        q_copy(QL, 7, q, False).wait_recv()
        got = QR[8, q] + QL[8, q] + mine[q]
        for i in range(NY):
            SB[q * NY + i] = got[i * BR : i * BR + BR]
        for i in range(NY):
            b = q * NY + i

            @pl.when(b != ip)
            def _():
                remote(SB.at[b], R.at[c, ip], a_s.at[b], a_r.at[ip], dev(b // 8, b % 8, z, c)).start()

    R[c, ip] = SB[ip]

    @pl.when(act)
    def _():
        tile = DR[0]
        for d in range(1, NZ):
            remote(DR.at[0], DR.at[d], dz_s.at[d], dz_r.at[d], mate).wait_recv()
            tile += DR[d]
        DO[...] = tile
        remote(DO, DO, do_s, do_r, mate).start()

    def group(core, d):
        b = R.at[core, pl.ds(lax.rem(x + d, NX) * NY, NY)]
        return remote(b, b, r_s.at[d], r_r.at[d], mate)

    for d in (0, 1, 3, 2):

        @pl.loop(0, NY)
        def _(yy):
            b = lax.rem(x + d, NX) * NY + yy

            @pl.when(b != ip)
            def _():
                remote(SB.at[b], R.at[c, b], a_s.at[b], a_r.at[b], mate).wait_recv()

        group(c, d).start()

    @pl.when(jnp.logical_not(act))
    def _():
        remote(DO, DO, do_s, do_r, mate).wait_recv()

    dens_out[...] = DO[...]

    @pl.when(home)
    def _():
        remote(bs.at[k], S.at[k, x, h, y], w_s.at[0], w_r.at[0], mate).wait_send()

    @pl.when(jnp.logical_not(home))
    def _():
        remote(bf, F.at[ja], f0_s, f0_r, mate).wait_send()
        remote(bs.at[c], S.at[c, x, h, y], w_s.at[0], w_r.at[1], mate).wait_send()
        remote(bs.at[k], S.at[k, x, h, y], w_s.at[1], w_r.at[1], mate).wait_send()

    for right in (True, False):
        ss = fr_s if right else fl_s
        for s in range(8 if right else 7):
            o = lax.rem(z + NZ - s, NZ) if right else lax.rem(z + s, NZ)

            @pl.when(o // 8 == c)
            def _():
                for q in range(4):
                    b = F.at[lax.rem(o, NL) * 2 + q // 2, pl.ds(q % 2 * 32, 32)]
                    remote(b, b, ss.at[s, q], fr_r.at[s, q], mate).wait_send()

    for slot in range(2):

        @pl.when(first)
        def _():
            for d in ROWS:
                along_y(piece(h), yr, slot, d, 1).wait_send()
            for d in LINES:
                along_x(line(h, x), lax.rem(x + 1, NX), slot, d, 2).wait_send()
            for n in range(NX):
                remote(line(h, x), line(h, x), pc_s.at[slot, n], pc_r.at[slot, n], mate).wait_send()

        @pl.when(jnp.logical_not(first))
        def _():
            for d in LINES:
                along_x(piece(h), lax.rem(x + 1, NX), slot, d, 1).wait_send()
            for d in ROWS:
                along_y(column(h, y), yr, slot, d, 2).wait_send()
            for n in range(NY):
                remote(column(h, y), column(h, y), pc_s.at[slot, n], pc_r.at[slot, n], mate).wait_send()

    for right, buf in ((True, QR), (False, QL)):
        for s in range(8):
            for q in EARLY[right] if s == 0 else range(4):
                q_copy(buf, s, q, right).wait_send()
    d_mate.wait_send()
    for d in range(1, NY):
        remote(D.at[c, :, 0], DY.at[d - 1], dy_s.at[d - 1], dy_r.at[d - 1], mate).wait_send()
    for i in range(2):

        @pl.when(2 * c + i != x)
        def _():
            remote(DX.at[0, i], DX.at[1, 0], dx_s.at[i], dx_r.at[1], mate).wait_send()

    @pl.when(act)
    def _():
        for d in range(1, NZ):
            remote(DR.at[0], DR.at[d], dz_s.at[d], dz_r.at[d], mate).wait_send()
        remote(DO, DO, do_s, do_r, mate).wait_send()

    @pl.loop(1, PLANE)
    def _(d):
        b = lax.rem(ip + d, PLANE)
        remote(SB.at[b], R.at[c, b], a_s.at[b], a_r.at[b], mate).wait_send()

    for d in range(NX):
        group(c, d).wait_send()
        group(k, d).wait_recv()


def last_kernel(r_hbm, co_hbm, dens, gamma_hbm, density, r, co, gamma, W, LT, L, sem, out_sem):
    _, _, _, l, c = place()
    co_in = pltpu.make_async_copy(co_hbm, co, sem.at[0])
    r_in = pltpu.make_async_copy(r_hbm, r, sem.at[1])
    co_in.start()
    r_in.start()
    W[...] = jnp.zeros_like(W)
    co_in.wait()
    for hi in range(2):
        for x in range(NX):
            rows = co[(x * 2 + hi) * 8 : (x * 2 + hi) * 8 + 8, :]
            at = hi * 32 + x * 8
            W[at : at + 8, 0:576] = rows
            W[64 + at : 64 + at + 8, 576:1152] = rows
    w_hi, w_lo = split(W[...])
    r_in.wait()
    for n in range(BR):
        LT[n] = jnp.transpose(r[:, :, n, :].reshape(64, 128))
        even = LT[n, pl.ds(c * 64, 32, stride=2), :]
        odd = LT[n, pl.ds(c * 64 + 1, 32, stride=2), :]
        L[pl.ds(n, 32, stride=16), :] = jnp.concatenate([even, odd], axis=1)
    outs = []
    for g in range(4):
        l_hi, l_lo = split(L[g * 128 : g * 128 + 128, :])
        res = dot(l_hi, w_hi, 1, 0) + dot(l_lo, w_hi, 1, 0) + dot(l_hi, w_lo, 1, 0)
        for t in range(8):
            at = (g * 8 + t) * 1152
            gamma[:, at : at + 1152] = res[t * 16 : t * 16 + BR, :]
        cols = pl.ds(g * 9216, 9216)
        outs.append(pltpu.make_async_copy(gamma.at[:, cols], gamma_hbm.at[:, cols], out_sem.at[g]))
        outs[-1].start()
    at = (l % 2) * 64 + c * 32
    turned = pltpu.roll(dens[...], lax.rem(128 - at, 128), 1)
    density[...] = turned[:, 0:32] * (1.0 / 2048.0)
    for copy in outs:
        copy.wait()


def on_device(b_first, b_second, eps_first, eps_second, eps_virtual, c_virtual, c_occupied):
    bf = jnp.swapaxes(b_first, 1, 2)[0]
    bs = jnp.swapaxes(b_second, 1, 2)
    dma = pltpu.SemaphoreType.DMA
    vm = pl.BlockSpec(memory_space=pltpu.VMEM)
    sm = pl.BlockSpec(memory_space=pltpu.SMEM)
    hb = pl.BlockSpec(memory_space=pltpu.HBM)
    r, dens = pl.pallas_call(
        main_kernel,
        out_shape=(
            jax.ShapeDtypeStruct((2, PLANE, BR, 128), F32),
            jax.ShapeDtypeStruct((8, 128), F32),
        ),
        in_specs=[hb, hb, sm, sm, hb, hb],
        out_specs=(vm, vm),
        scratch_shapes=[
            pltpu.VMEM((1, 512), F32),
            pltpu.VMEM((8, CR, 512), F32),
            pltpu.VMEM((16, 64, 512), BF16),
            pltpu.VMEM((2, NX, NH, NY, 16, 512), BF16),
            pltpu.VMEM((3, 3, 8, 128), F32),
            pltpu.VMEM((NH, 2, 144, 512), BF16),
            pltpu.VMEM((NH, 2, 144, 512), BF16),
            pltpu.VMEM((2, 512, 512), BF16),
            pltpu.VMEM((2, 512, 512), BF16),
            pltpu.VMEM((8, 512, 128), F32),
            pltpu.VMEM((8, 512, 256), BF16),
            pltpu.VMEM((2, 4, 8, 8, 512), F32),
            pltpu.VMEM((4, 8, 8, 512), F32),
            pltpu.VMEM((7, 4, 8, 512), F32),
            pltpu.VMEM((4, 2, 2, 8, 512), F32),
            pltpu.VMEM((2, 4, 8, 128), F32),
            pltpu.VMEM((16, 8, 128), F32),
            pltpu.VMEM((8, 128), F32),
            pltpu.VMEM((9, 4, CR, 128), F32),
            pltpu.VMEM((9, 4, CR, 128), F32),
            pltpu.VMEM((PLANE, BR, 128), F32),
            dma, dma, dma((8, 4)), dma((8, 4)), dma((7, 4)), dma((7, 4)),
            dma((2,)), dma((2,)), dma((2, 4)), dma((2, 4)), dma((2, 4)), dma((2, 4)),
            dma((2, 8)), dma((2, 8)), dma((2, 8)), dma((2, 8)), dma((2, 8)), dma((2, 8)),
            dma((2,)), dma((2,)),
            dma((8, 4)), dma((8, 4)), dma((8, 4)), dma((8, 4)), dma, dma, dma((7,)), dma((7,)),
            dma((2,)), dma((4,)), dma((16,)), dma((16,)), dma, dma,
            dma((PLANE,)), dma((PLANE,)), dma((NX,)), dma((NX,)), dma((4,)),
        ],
        compiler_params=pltpu.CompilerParams(
            collective_id=0, has_side_effects=True, vmem_limit_bytes=66_560_000
        ),
        name="pairs",
    )(bf, bs, eps_first, eps_second, eps_virtual.reshape(1, 512), c_virtual.reshape(8, CR, 512))
    return pl.pallas_call(
        last_kernel,
        out_shape=(
            jax.ShapeDtypeStruct((BR, 36864), F32),
            jax.ShapeDtypeStruct((8, 32), F32),
        ),
        in_specs=[hb, hb, vm],
        out_specs=(hb, vm),
        scratch_shapes=[
            pltpu.VMEM((2, PLANE, BR, 128), F32),
            pltpu.VMEM((64, 576), F32),
            pltpu.VMEM((BR, 36864), F32),
            pltpu.VMEM((128, 1152), F32),
            pltpu.VMEM((BR, 128, 64), F32),
            pltpu.VMEM((512, 128), F32),
            dma((2,)),
            dma((4,)),
        ],
        compiler_params=pltpu.CompilerParams(vmem_limit_bytes=66_560_000),
        name="last",
    )(r, c_occupied, dens)


def solution(mesh):
    return jax.shard_map(
        on_device,
        mesh=mesh,
        in_specs=(P("ia", None, "ja"), P("ja", None, "ia"), P("ia"), P("ja"), P(), P(), P()),
        out_specs=(P("ia", "ja"), P("ia", "ja")),
        check_vma=False,
    )
```
